512 devices in a mesh: dp: 16 (over y, core), context: 32 (over z, x).
Axes of the slice: x: 4, y: 8, z: 8, core: 2. Of those that a mesh axis runs over, the one named last changes fastest.
Arguments:
- queries: bfloat16 [16, 4096, 2048], P('dp', 'context'), may hold values from -6 to 6
- keys: bfloat16 [16, 4096, 2048], P('dp', 'context'), may hold values from -6 to 6
- values: bfloat16 [16, 4096, 2048], P('dp', 'context'), may hold values from -6 to 6
- out_grad: bfloat16 [16, 4096, 2048], P('dp', 'context'), may hold values from -6 to 6
- log_gates: float32 [16, 16, 4096], P('dp', None, 'context'), may hold values from -1 to 0, as said below
- query_map: bfloat16 [16, 128, 128], replicated, may hold values from -0.5 to 0.5
- key_map: bfloat16 [16, 128, 128], replicated, may hold values from -0.5 to 0.5
Outputs:
- query_grad: bfloat16 [16, 4096, 2048], P('dp', 'context')
- key_grad: bfloat16 [16, 4096, 2048], P('dp', 'context')
- value_grad: bfloat16 [16, 4096, 2048], P('dp', 'context')
- map_grads: float32 [4096, 128], P(('dp', 'context'))
The draws below stay inside these ranges and needn't reach their ends.
Inputs may be any that keep to these rules, and one draw needn't show every extreme that they name: `log_gates`: every entry is negative.
All inputs are finite; a program needn't handle non-finite values.
Results may differ from the reference program's by a relative error of at most 0.019.
Values may be sent and summed in bfloat16 or wider, within the bound.
No kernel may reach another device: no remote copies, remote signals or barrier semaphores. Data moves between devices by JAX's collectives and lax.ppermute only.
A program may use at most 128 MiB of HBM per device.

```python
import math
import jax
import jax.numpy as jnp
from jax import lax

LOCAL_HEADS = 16
DH = 128
TOK_DEV = 128
BATCH_SEQUENCES = 16
SEQUENCE_LENGTH = 4096
TOKENS = 65536


def draw_log_gates(key, part):
    gathered_keys = jax.random.split(key, 7)
    picker = jax.random.uniform(gathered_keys[0], (BATCH_SEQUENCES, LOCAL_HEADS, 1))
    fast = picker < 0.5
    fast_rate = math.log(10.0) / jnp.exp(jax.random.uniform(gathered_keys[1], (BATCH_SEQUENCES, LOCAL_HEADS, 1), minval=math.log(30.0), maxval=math.log(50.0)))
    slow_rate = 0.15 * math.log(10.0) / SEQUENCE_LENGTH * jax.random.uniform(gathered_keys[2], (BATCH_SEQUENCES, LOCAL_HEADS, 1), minval=0.5, maxval=1.0)
    rate = jnp.where(fast, fast_rate, slow_rate)
    block_factor = jnp.exp(jax.random.uniform(gathered_keys[3], (BATCH_SEQUENCES, LOCAL_HEADS, SEQUENCE_LENGTH // TOK_DEV), minval=-0.7, maxval=0.7))
    factor = jnp.repeat(block_factor, TOK_DEV, axis=2)
    jitter = jax.random.uniform(gathered_keys[4], (BATCH_SEQUENCES, LOCAL_HEADS, SEQUENCE_LENGTH), minval=0.5, maxval=1.5)
    drawn_gates = -rate * factor * jitter
    token_spots = jax.random.randint(gathered_keys[5], (BATCH_SEQUENCES, LOCAL_HEADS, 2), 0, SEQUENCE_LENGTH)
    token_place = jnp.arange(SEQUENCE_LENGTH)[None, None, :]
    spike_mask = (token_place == token_spots[:, :, 0:1]) | (token_place == token_spots[:, :, 1:2])
    spike_gates = jnp.log(jax.random.uniform(gathered_keys[6], (BATCH_SEQUENCES, LOCAL_HEADS, SEQUENCE_LENGTH), minval=0.5, maxval=0.8))
    return (drawn_gates + jnp.where(spike_mask, spike_gates, 0.0)).astype(jnp.float32)


def shard_levels(own_key, shape, pieces, least, high):
    def one(dim, parts):
        draws = jax.random.uniform(jax.random.fold_in(jax.random.fold_in(own_key, 6), dim), (parts,), jnp.float32, least / len(pieces), high / len(pieces))
        return jnp.repeat(jnp.exp(draws), shape[dim] // parts).reshape((-1,) + (1,) * (len(shape) - dim - 1))

    gain = one(*pieces[0])
    for cut in pieces[1:]:
        gain = gain * one(*cut)
    return gain


def centred(stream_key, extent, width, reach, shards=(), kind=jnp.bfloat16):
    values = width * jax.random.normal(stream_key, extent, jnp.float32)
    if shards:
        values = values * shard_levels(stream_key, extent, shards, -0.22, 0.18)
    return jnp.clip(values, -reach, reach).astype(kind)


def setup_inputs(seed: int = 0) -> dict:
    key_list = jax.random.split(jax.random.key(seed), 8)
    queries = centred(key_list[0], (BATCH_SEQUENCES, SEQUENCE_LENGTH, LOCAL_HEADS * DH), 1.0, 6.0, ((0, 16), (1, 32)))
    keys = centred(key_list[1], (BATCH_SEQUENCES, SEQUENCE_LENGTH, LOCAL_HEADS * DH), 1.0, 6.0, ((0, 16), (1, 32)))
    values = centred(key_list[2], (BATCH_SEQUENCES, SEQUENCE_LENGTH, LOCAL_HEADS * DH), 1.0, 6.0, ((0, 16), (1, 32)))
    out_grad = centred(key_list[3], (BATCH_SEQUENCES, SEQUENCE_LENGTH, LOCAL_HEADS * DH), 1.0, 6.0, ((0, 16), (1, 32)))
    log_gates = draw_log_gates(jax.random.fold_in(key_list[7], 71), 0)
    query_map = centred(key_list[5], (LOCAL_HEADS, DH, DH), DH ** -0.5, 0.5)
    key_map = centred(key_list[6], (LOCAL_HEADS, DH, DH), DH ** -0.5, 0.5)
    return dict(queries=queries, keys=keys, values=values, out_grad=out_grad, log_gates=log_gates, query_map=query_map, key_map=key_map)


exact_mode = lax.Precision.HIGHEST


def rounded(array):
    return lax.optimization_barrier(array.astype(jnp.bfloat16)).astype(jnp.float32)


def decay_tables(gates):
    running = jnp.cumsum(gates, axis=2)
    closing = running[:, :, -1]
    length = gates.shape[2]
    causal = jnp.arange(length)[:, None] >= jnp.arange(length)[None, :]
    spread = running[:, :, :, None] - running[:, :, None, :]
    within = jnp.where(causal, jnp.exp(jnp.where(causal, spread, 0.0)), 0.0)
    to_end = jnp.exp(closing[:, :, None] - running)
    from_start = jnp.exp(running)
    return within, to_end, from_start, jnp.exp(rounded(closing))


def reference(queries, keys, values, out_grad, log_gates, query_map, key_map):
    spans = SEQUENCE_LENGTH // TOK_DEV
    key_scale = DH ** -0.5 / 16.0
    map_query = query_map.astype(jnp.float32)
    map_key = key_map.astype(jnp.float32)

    def one_sequence(items):
        query_seq, key_seq, value_seq, grad_seq, gate_seq = items
        shape = (spans, TOK_DEV, LOCAL_HEADS, DH)
        query_heads = query_seq.reshape(shape).astype(jnp.float32)
        key_heads = key_seq.reshape(shape).astype(jnp.float32)
        value_heads = value_seq.reshape(shape).astype(jnp.float32)
        grad_heads = grad_seq.reshape(shape).astype(jnp.float32)
        gates = gate_seq.reshape(LOCAL_HEADS, spans, TOK_DEV).transpose(1, 0, 2)
        query_feat = rounded(jnp.einsum("btha,had->bthd", query_heads, map_query))
        key_feat = rounded(jnp.einsum("btha,had->bthd", key_heads, map_key) * key_scale)
        within, to_end, from_start, decay = decay_tables(gates)
        scores = rounded(jnp.einsum("bthd,bshd->bhts", query_feat, key_feat) * within)
        grad_scores = rounded(jnp.einsum("bthd,bshd->bhts", grad_heads, value_heads) * within)
        states_local = rounded(jnp.einsum("bshi,bhs,bshj->bhij", key_feat, to_end, value_heads, precision=exact_mode))
        grads_local = rounded(jnp.einsum("bthi,bht,bthj->bhij", query_feat, from_start, grad_heads, precision=exact_mode))

        def carry_on(carry, item):
            factor, block = item
            return factor[:, None, None] * carry + block, carry

        anchor = jnp.zeros((LOCAL_HEADS, DH, DH), jnp.float32)
        _, state_in = lax.scan(carry_on, anchor, (decay, states_local))
        _, grad_in = lax.scan(carry_on, anchor, (decay, grads_local), reverse=True)
        state_in = rounded(state_in)
        grad_in = rounded(grad_in)
        start_weight = jnp.transpose(from_start, (0, 2, 1))[..., None]
        end_weight = jnp.transpose(to_end, (0, 2, 1))[..., None]
        query_total = jnp.einsum("bhts,bshd->bthd", grad_scores, key_feat) + jnp.einsum("bthj,bhij->bthi", grad_heads, state_in, precision=exact_mode) * start_weight
        key_total = jnp.einsum("bhts,bthd->bshd", grad_scores, query_feat) + jnp.einsum("bshj,bhij->bshi", value_heads, grad_in, precision=exact_mode) * end_weight
        value_total = jnp.einsum("bhts,bthd->bshd", scores, grad_heads) + jnp.einsum("bshi,bhij->bshj", key_feat, grad_in, precision=exact_mode) * end_weight
        query_back = rounded(query_total)
        key_back = rounded(key_total * key_scale)
        query_out = jnp.einsum("bthd,had->btha", query_back, map_query).astype(jnp.bfloat16).reshape(SEQUENCE_LENGTH, LOCAL_HEADS * DH)
        key_out = jnp.einsum("bthd,had->btha", key_back, map_key).astype(jnp.bfloat16).reshape(SEQUENCE_LENGTH, LOCAL_HEADS * DH)
        value_out = value_total.astype(jnp.bfloat16).reshape(SEQUENCE_LENGTH, LOCAL_HEADS * DH)
        map_part = jnp.stack([jnp.einsum("btha,bthd->had", query_heads, query_back), jnp.einsum("btha,bthd->had", key_heads, key_back)])
        return query_out, key_out, value_out, map_part

    results = lax.map(one_sequence, (queries, keys, values, out_grad, log_gates))
    map_grads = (jnp.sum(results[3], axis=0) * (TOKENS ** -0.5)).reshape(2 * LOCAL_HEADS * DH, DH)
    return results[0], results[1], results[2], map_grads
```

```python
import functools

import jax
import jax.numpy as jnp
from jax import lax
from jax.experimental import pallas as pl
from jax.experimental.pallas import tpu as pltpu
from jax.sharding import PartitionSpec as P

F32 = jnp.float32
BF16 = jnp.bfloat16
GROUP = 8
PAD = 8


def dot(a, b, contract, precision=None):
    return lax.dot_general(
        a, b, ((contract[:1], contract[1:]), ((), ())), precision=precision, preferred_element_type=F32
    )


def running_tables(gates):
    length = gates.shape[1]
    t = lax.broadcasted_iota(jnp.int32, (length, length), 0)
    s = lax.broadcasted_iota(jnp.int32, (length, length), 1)
    causal = t >= s
    lower = jnp.where(causal, 1.0, 0.0).astype(F32)
    rows = dot(gates, lower, (1, 1), lax.Precision.HIGHEST)
    columns = dot(lower, gates, (1, 1), lax.Precision.HIGHEST)
    return causal, rows, columns


def states_kernel(key_scale, q_ref, k_ref, v_ref, g_ref, gates_ref, mq_ref, mk_ref, fq_ref, fk_ref, out_ref):
    width = mq_ref.shape[1]
    length = q_ref.shape[0]
    half = width // 2
    _, _, columns = running_tables(gates_ref[...])
    for j in range(GROUP):
        lanes = slice(j * width, (j + 1) * width)
        run = columns[:, j : j + 1]
        closing = run[length - 1 : length]
        fq = dot(q_ref[:, lanes], mq_ref[j], (1, 0)).astype(BF16)
        fk = (dot(k_ref[:, lanes], mk_ref[j], (1, 0)) * key_scale).astype(BF16)
        fq_ref[:, lanes] = fq
        fk_ref[:, lanes] = fk
        fk_end = (fk.astype(F32) * jnp.exp(closing - run)).astype(BF16)
        fq_start = (fq.astype(F32) * jnp.exp(run)).astype(BF16)
        state = dot(fk_end, v_ref[:, lanes], (0, 0)).astype(BF16)
        grad = dot(fq_start, g_ref[:, lanes], (0, 0)).astype(BF16)
        log = jnp.broadcast_to(closing, (PAD, width)).astype(BF16)
        for part in range(2):
            rows = slice(part * half, (part + 1) * half)
            out_ref[2 * j + part, 0:half] = state[rows]
            out_ref[2 * j + part, half:width] = grad[rows]
            out_ref[2 * j + part, width : width + PAD] = log


def scan_kernel(in_ref, out_ref):
    blocks, width = in_ref.shape[0], in_ref.shape[2]
    half = width // 2

    def step(carry, at, low):
        out_ref[at, low : low + half] = carry.reshape(half, width).astype(BF16)
        decay = jnp.exp(in_ref[at, width : width + PAD].astype(F32))
        new = in_ref[at, low : low + half].astype(F32).reshape(half // PAD, PAD, width)
        return decay[None] * carry + new

    zero = jnp.zeros((half // PAD, PAD, width), F32)
    ahead, back = zero, zero
    for c in range(blocks):
        ahead = step(ahead, c, 0)
        back = step(back, blocks - 1 - c, half)


def grads_kernel(
    key_scale, map_scale, q_ref, k_ref, v_ref, g_ref, fq_ref, fk_ref, gates_ref, mq_ref, mk_ref, in_ref,
    qg_ref, kg_ref, vg_ref, maps_ref,
):
    width = mq_ref.shape[1]
    length = q_ref.shape[0]
    half = width // 2
    causal, rows, columns = running_tables(gates_ref[...])
    for j in range(GROUP):
        lanes = slice(j * width, (j + 1) * width)
        run = columns[:, j : j + 1]
        closing = run[length - 1 : length]
        start = jnp.exp(run)
        end = jnp.exp(closing - run)
        within = jnp.exp(jnp.where(causal, run - rows[j : j + 1], -1e30))
        q, k, v, g = q_ref[:, lanes], k_ref[:, lanes], v_ref[:, lanes], g_ref[:, lanes]
        fq, fk = fq_ref[:, lanes], fk_ref[:, lanes]
        state_in = jnp.concatenate([in_ref[2 * j, 0:half], in_ref[2 * j + 1, 0:half]], axis=0)
        grad_in = jnp.concatenate([in_ref[2 * j, half:width], in_ref[2 * j + 1, half:width]], axis=0)
        scores = (dot(fq, fk, (1, 1)) * within).astype(BF16)
        grad_scores = (dot(g, v, (1, 1)) * within).astype(BF16)
        query_back = (dot(grad_scores, fk, (1, 0)) + dot(g, state_in, (1, 1)) * start).astype(BF16)
        key_back = (
            (dot(grad_scores, fq, (0, 0)) + dot(v, grad_in, (1, 1)) * end) * key_scale
        ).astype(BF16)
        value_grad = dot(scores, g, (0, 0)) + dot(fk, grad_in, (1, 0)) * end
        vg_ref[:, lanes] = value_grad.astype(BF16)
        qg_ref[:, lanes] = dot(query_back, mq_ref[j], (1, 1)).astype(BF16)
        kg_ref[:, lanes] = dot(key_back, mk_ref[j], (1, 1)).astype(BF16)
        core, where, y = (j // 2) % 2, (j % 2) * (width // 8), j // 4
        for m, (x, back) in enumerate(((q, query_back), (k, key_back))):
            part = (dot(x, back, (0, 0)) * map_scale).astype(BF16)
            maps_ref[core, where : where + width // 8, m, y] = part.reshape(width // 8, 8, width)


def sum_kernel(in_ref, out_ref):
    out_ref[...] = jnp.sum(in_ref[...].astype(F32), axis=0).astype(out_ref.dtype)


def add_up(value, dtype):
    return pl.pallas_call(sum_kernel, out_shape=jax.ShapeDtypeStruct(value.shape[1:], dtype))(value)


def exchange(value, axis, groups=None):
    return lax.all_to_all(value, axis, 0, 0, axis_index_groups=groups, tiled=True)


def per_device(queries, keys, values, out_grad, log_gates, query_map, key_map):
    heads, width = query_map.shape[0], query_map.shape[1]
    length = queries.shape[1]
    dp, context = lax.axis_size("dp"), lax.axis_size("context")
    key_scale = width ** (-0.5) / 16.0
    map_scale = (dp * context * length) ** (-0.5)
    steps = heads // GROUP
    q, k, v, g = (x.reshape(length, heads * width) for x in (queries, keys, values, out_grad))
    gates = log_gates.reshape(heads, length)
    wide = pl.BlockSpec((length, GROUP * width), lambda i: (0, i))
    gate_spec = pl.BlockSpec((GROUP, length), lambda i: (i, 0))
    map_spec = pl.BlockSpec((GROUP, width, width), lambda i: (i, 0, 0))
    wide_shape = jax.ShapeDtypeStruct((length, heads * width), BF16)
    fq, fk, sent = pl.pallas_call(
        functools.partial(states_kernel, key_scale),
        grid=(steps,),
        in_specs=[wide, wide, wide, wide, gate_spec, map_spec, map_spec],
        out_specs=[wide, wide, pl.BlockSpec((2 * GROUP, width + PAD, width), lambda i: (i, 0, 0))],
        out_shape=[wide_shape, wide_shape, jax.ShapeDtypeStruct((2 * heads, width + PAD, width), BF16)],
    )(q, k, v, g, gates, query_map, key_map)
    received = exchange(sent, "context")
    scanned = pl.pallas_call(
        scan_kernel,
        out_shape=jax.ShapeDtypeStruct((context, width, width), BF16),
    )(received)
    carried = exchange(scanned, "context")
    query_grad, key_grad, value_grad, maps = pl.pallas_call(
        functools.partial(grads_kernel, key_scale, map_scale),
        grid=(steps,),
        in_specs=[wide] * 6 + [gate_spec, map_spec, map_spec]
        + [pl.BlockSpec((2 * GROUP, width, width), lambda i: (i, 0, 0))],
        out_specs=[wide, wide, wide, pl.BlockSpec((2, 32, 2, 2, 8, width), lambda i: (0, 0, 0, i, 0, 0))],
        out_shape=[wide_shape] * 3 + [jax.ShapeDtypeStruct((2, 32, 2, heads // 4, 8, width), BF16)],
    )(q, k, v, g, fq, fk, gates, query_map, key_map, carried)
    cores = [[2 * y, 2 * y + 1] for y in range(dp // 2)]
    chips = [[2 * y + c for y in range(dp // 2)] for c in range(2)]
    maps = exchange(maps, "dp", cores)
    maps = exchange(add_up(maps, BF16), "context")
    maps = exchange(add_up(maps, BF16).reshape(dp // 2, 8, width), "dp", chips)
    map_grads = add_up(maps, F32)
    whole = queries.shape
    return query_grad.reshape(whole), key_grad.reshape(whole), value_grad.reshape(whole), map_grads


def solution(mesh):
    split = P("dp", "context", None)
    return jax.shard_map(
        per_device,
        mesh=mesh,
        in_specs=(split, split, split, split, P("dp", None, "context"), P(), P()),
        out_specs=(split, split, split, P(("dp", "context"), None)),
        check_vma=False,
    )
```

```python
import functools

import jax
import jax.numpy as jnp
import numpy as np
from jax import lax
from jax.experimental import pallas as pl
from jax.experimental.pallas import tpu as pltpu
from jax.sharding import Mesh, PartitionSpec as P

F32 = jnp.float32
BF16 = jnp.bfloat16
GROUP = 8
PAD = 8
VMEM = pltpu.CompilerParams(vmem_limit_bytes=20 << 20)
DP = ("y_hi", "y_lo", "core")
CONTEXT = ("outer", "inner", "x")
NEAR = ("inner", "x")
FIRST, SECOND = ("y_lo", "core", "inner", "x"), ("y_hi", "outer")


def dot(a, b, contract, precision=None):
    return lax.dot_general(
        a, b, ((contract[:1], contract[1:]), ((), ())), precision=precision, preferred_element_type=F32
    )


def causal_mask(length):
    t = lax.broadcasted_iota(jnp.int32, (length, length), 0)
    s = lax.broadcasted_iota(jnp.int32, (length, length), 1)
    return t >= s


def running_columns(gates):
    lower = jnp.where(causal_mask(gates.shape[1]), 1.0, 0.0).astype(F32)
    return dot(lower, gates, (1, 1), lax.Precision.HIGHEST)


def running_rows(gates):
    lower = jnp.where(causal_mask(gates.shape[1]), 1.0, 0.0).astype(F32)
    return dot(gates, lower, (1, 1), lax.Precision.HIGHEST)


def states_kernel(key_scale, q_ref, k_ref, v_ref, g_ref, gates_ref, mq_ref, mk_ref, fq_ref, fk_ref, out_ref):
    width = mq_ref.shape[1]
    length = q_ref.shape[0]
    columns = running_columns(gates_ref[...])
    for j in range(GROUP):
        lanes = slice(j * width, (j + 1) * width)
        run = columns[:, j : j + 1]
        closing = run[length - 1 : length]
        fq = dot(q_ref[:, lanes], mq_ref[j], (1, 0)).astype(BF16)
        fk = (dot(k_ref[:, lanes], mk_ref[j], (1, 0)) * key_scale).astype(BF16)
        fq_ref[:, lanes] = fq
        fk_ref[:, lanes] = fk
        fk_end = (fk.astype(F32) * jnp.exp(closing - run)).astype(BF16)
        fq_start = (fq.astype(F32) * jnp.exp(run)).astype(BF16)
        out_ref[j, 0:width] = dot(fk_end, v_ref[:, lanes], (0, 0)).astype(BF16)
        out_ref[j, width : 2 * width] = dot(fq_start, g_ref[:, lanes], (0, 0)).astype(BF16)
        out_ref[j, 2 * width :] = jnp.broadcast_to(closing, (PAD, width)).astype(BF16)


def inside_kernel(key_scale, v_ref, g_ref, fq_ref, fk_ref, gates_ref, qb_ref, kb_ref, vg_ref):
    length = v_ref.shape[0]
    width = v_ref.shape[1] // GROUP
    causal = causal_mask(length)
    columns = running_columns(gates_ref[...])
    rows = running_rows(gates_ref[...])
    for j in range(GROUP):
        lanes = slice(j * width, (j + 1) * width)
        within = jnp.exp(jnp.where(causal, columns[:, j : j + 1] - rows[j : j + 1], -1e30))
        v, g, fq, fk = v_ref[:, lanes], g_ref[:, lanes], fq_ref[:, lanes], fk_ref[:, lanes]
        scores = (dot(fq, fk, (1, 1)) * within).astype(BF16)
        grad_scores = (dot(g, v, (1, 1)) * within).astype(BF16)
        qb_ref[:, lanes] = dot(grad_scores, fk, (1, 0))
        kb_ref[:, lanes] = dot(grad_scores, fq, (0, 0))
        vg_ref[:, lanes] = dot(scores, g, (0, 0))


def over(decay, value):
    rows, width = value.shape
    return (decay[None] * value.reshape(rows // PAD, PAD, width)).reshape(rows, width)


def totals_kernel(in_ref, out_ref):
    near, heads, width = in_ref.shape[0], in_ref.shape[1], in_ref.shape[3]
    mine = lax.axis_index("outer")
    for h in range(heads):
        ahead = jnp.zeros((width, width), F32)
        back = jnp.zeros((width, width), F32)
        log = jnp.zeros((PAD, width), F32)
        for r in range(near):
            b = near - 1 - r
            ahead = over(jnp.exp(in_ref[r, h, 2 * width :].astype(F32)), ahead) + in_ref[r, h, 0:width].astype(F32)
            back = over(jnp.exp(in_ref[b, h, 2 * width :].astype(F32)), back) + in_ref[
                b, h, width : 2 * width
            ].astype(F32)
            log = log + in_ref[r, h, 2 * width :].astype(F32)
        coarse = log.astype(BF16)
        fine = (log - coarse.astype(F32)).astype(BF16)
        for o in range(out_ref.shape[0]):
            out_ref[o, h, 0:width] = jnp.where(o > mine, ahead, back).astype(BF16)
            out_ref[o, h, width : width + PAD] = coarse
            out_ref[o, h, width + PAD :] = fine


def spread_kernel(in_ref, totals_ref, out_ref):
    near, heads, width = in_ref.shape[0], in_ref.shape[1], in_ref.shape[3]
    groups = totals_ref.shape[0]
    mine = lax.axis_index("outer")

    def total(o, h):
        log = totals_ref[o, h, width : width + PAD].astype(F32) + totals_ref[o, h, width + PAD :].astype(F32)
        return jnp.exp(log), totals_ref[o, h, 0:width].astype(F32)

    for h in range(heads):
        ahead = jnp.zeros((width, width), F32)
        back = jnp.zeros((width, width), F32)
        for o in range(groups):
            decay, value = total(o, h)
            ahead = jnp.where(o < mine, over(decay, ahead) + value, ahead)
            b = groups - 1 - o
            decay, value = total(b, h)
            back = jnp.where(b > mine, over(decay, back) + value, back)
        for r in range(near):
            b = near - 1 - r
            out_ref[r, h, 0:width] = ahead.astype(BF16)
            out_ref[b, h, width : 2 * width] = back.astype(BF16)
            if r < near - 1:
                ahead = over(jnp.exp(in_ref[r, h, 2 * width :].astype(F32)), ahead) + in_ref[r, h, 0:width].astype(F32)
                back = over(jnp.exp(in_ref[b, h, 2 * width :].astype(F32)), back) + in_ref[
                    b, h, width : 2 * width
                ].astype(F32)


def backs_kernel(
    key_scale, map_scale, q_ref, k_ref, v_ref, g_ref, gates_ref, qbi_ref, kbi_ref, in_ref, qb_ref, kb_ref, maps_ref
):
    length = q_ref.shape[0]
    width = q_ref.shape[1] // GROUP
    columns = running_columns(gates_ref[...])
    for j in range(GROUP):
        lanes = slice(j * width, (j + 1) * width)
        run = columns[:, j : j + 1]
        start = jnp.exp(run)
        end = jnp.exp(run[length - 1 : length] - run)
        state_in, grad_in = in_ref[j, 0:width], in_ref[j, width:]
        query_back = (qbi_ref[:, lanes] + dot(g_ref[:, lanes], state_in, (1, 1)) * start).astype(BF16)
        key_back = ((kbi_ref[:, lanes] + dot(v_ref[:, lanes], grad_in, (1, 1)) * end) * key_scale).astype(BF16)
        qb_ref[:, lanes] = query_back
        kb_ref[:, lanes] = key_back
        for m, (x, back) in enumerate(((q_ref[:, lanes], query_back), (k_ref[:, lanes], key_back))):
            part = dot(x, back, (0, 0)) * map_scale
            for b in range(width // 8):
                to = (j // 2) * 8 + b % 8
                maps_ref[to, m, 0, (j % 2) * 2 + b // 8] = part[8 * b : 8 * b + 8].astype(BF16)


def grads_kernel(fk_ref, gates_ref, mq_ref, mk_ref, qb_ref, kb_ref, vgi_ref, in_ref, qg_ref, kg_ref, vg_ref):
    width = mq_ref.shape[1]
    length = fk_ref.shape[0]
    columns = running_columns(gates_ref[...])
    for j in range(GROUP):
        lanes = slice(j * width, (j + 1) * width)
        run = columns[:, j : j + 1]
        end = jnp.exp(run[length - 1 : length] - run)
        vg_ref[:, lanes] = (vgi_ref[:, lanes] + dot(fk_ref[:, lanes], in_ref[j, width:], (1, 0)) * end).astype(BF16)
        qg_ref[:, lanes] = dot(qb_ref[:, lanes], mq_ref[j], (1, 1)).astype(BF16)
        kg_ref[:, lanes] = dot(kb_ref[:, lanes], mk_ref[j], (1, 1)).astype(BF16)


def sum_kernel(in_ref, out_ref):
    out_ref[...] = jnp.sum(in_ref[...].astype(F32), axis=0).astype(out_ref.dtype)


def add_up(value, dtype):
    out_shape = jax.ShapeDtypeStruct(value.shape[1:], dtype)
    return pl.pallas_call(sum_kernel, out_shape=out_shape, compiler_params=VMEM)(value)


def exchange(value, axes):
    return lax.all_to_all(value, axes, 0, 0, tiled=True)


def per_device(queries, keys, values, out_grad, log_gates, query_map, key_map):
    heads, width = query_map.shape[0], query_map.shape[1]
    length = queries.shape[1]
    near, outer = lax.axis_size(NEAR), lax.axis_size("outer")
    key_scale = width ** (-0.5) / 16.0
    map_scale = (lax.axis_size(DP) * lax.axis_size(CONTEXT) * length) ** (-0.5)
    steps = heads // GROUP
    share = heads // near
    q, k, v, g = (x.reshape(length, heads * width) for x in (queries, keys, values, out_grad))
    gates = log_gates.reshape(heads, length)
    wide = pl.BlockSpec((length, GROUP * width), lambda i: (0, i))
    gate_spec = pl.BlockSpec((GROUP, length), lambda i: (i, 0))
    map_spec = pl.BlockSpec((GROUP, width, width), lambda i: (i, 0, 0))
    wide_shape = jax.ShapeDtypeStruct((length, heads * width), BF16)
    sum_shape = jax.ShapeDtypeStruct((length, heads * width), F32)
    flops = 2 * length * width * width * heads
    fq, fk, sent = pl.pallas_call(
        functools.partial(states_kernel, key_scale),
        grid=(steps,),
        in_specs=[wide, wide, wide, wide, gate_spec, map_spec, map_spec],
        out_specs=[wide, wide, pl.BlockSpec((GROUP, 2 * width + PAD, width), lambda i: (i, 0, 0))],
        out_shape=[wide_shape, wide_shape, jax.ShapeDtypeStruct((heads, 2 * width + PAD, width), BF16)],
        cost_estimate=pl.CostEstimate(flops=4 * flops, bytes_accessed=6 << 20, transcendentals=0),
    )(q, k, v, g, gates, query_map, key_map)
    received = exchange(sent.reshape(near, share, 2 * width + PAD, width), NEAR)
    inside = pl.pallas_call(
        functools.partial(inside_kernel, key_scale),
        grid=(steps,),
        in_specs=[wide] * 4 + [gate_spec],
        out_specs=[wide] * 3,
        out_shape=[sum_shape] * 3,
        cost_estimate=pl.CostEstimate(flops=5 * flops, bytes_accessed=6 << 20, transcendentals=1 << 18),
    )(v, g, fq, fk, gates)
    totals = pl.pallas_call(
        totals_kernel,
        out_shape=jax.ShapeDtypeStruct((outer, share, width + 2 * PAD, width), BF16),
        compiler_params=VMEM,
    )(received)
    totals = exchange(totals, "outer")
    spread = pl.pallas_call(
        spread_kernel,
        out_shape=jax.ShapeDtypeStruct((near, share, 2 * width, width), BF16),
        compiler_params=VMEM,
    )(received, totals)
    carried = exchange(spread, NEAR).reshape(heads, 2 * width, width)
    carried_spec = pl.BlockSpec((GROUP, 2 * width, width), lambda i: (i, 0, 0))
    query_back, key_back, maps = pl.pallas_call(
        functools.partial(backs_kernel, key_scale, map_scale),
        grid=(steps,),
        in_specs=[wide] * 4 + [gate_spec] + [wide] * 2 + [carried_spec],
        out_specs=[wide] * 2 + [pl.BlockSpec((32, 2, 1, 4, 8, width), lambda i: (0, 0, i, 0, 0, 0))],
        out_shape=[wide_shape] * 2 + [jax.ShapeDtypeStruct((32, 2, steps, 4, 8, width), BF16)],
        cost_estimate=pl.CostEstimate(flops=4 * flops, bytes_accessed=7 << 20, transcendentals=0),
    )(q, k, v, g, gates, inside[0], inside[1], carried)
    maps = exchange(maps.reshape(32, 16, 8, width), FIRST)
    query_grad, key_grad, value_grad = pl.pallas_call(
        grads_kernel,
        grid=(steps,),
        in_specs=[wide, gate_spec, map_spec, map_spec] + [wide] * 3 + [carried_spec],
        out_specs=[wide] * 3,
        out_shape=[wide_shape] * 3,
        cost_estimate=pl.CostEstimate(flops=3 * flops, bytes_accessed=6 << 20, transcendentals=0),
    )(fk, gates, query_map, key_map, query_back, key_back, inside[2], carried)
    maps = exchange(add_up(maps, BF16), SECOND)
    map_grads = add_up(maps, F32)
    whole = queries.shape
    return query_grad.reshape(whole), key_grad.reshape(whole), value_grad.reshape(whole), map_grads


def solution(mesh):
    fine = Mesh(np.asarray(mesh.devices).reshape(4, 2, 2, 4, 2, 4), DP + CONTEXT)
    split = P(DP, CONTEXT, None)
    return jax.shard_map(
        per_device,
        mesh=fine,
        in_specs=(split, split, split, split, P(DP, None, CONTEXT), P(), P()),
        out_specs=(split, split, split, P(DP + CONTEXT, None)),
        check_vma=False,
    )
```

```python
import functools

import jax
import jax.numpy as jnp
import numpy as np
from jax import lax
from jax.experimental import pallas as pl
from jax.experimental.pallas import tpu as pltpu
from jax.sharding import Mesh, PartitionSpec as P

F32 = jnp.float32
BF16 = jnp.bfloat16
GROUP = 8
PAD = 8
DP = ("y", "core")
CONTEXT = ("outer", "inner", "x")
NEAR = ("inner", "x")
VMEM = pltpu.CompilerParams(vmem_limit_bytes=20 << 20)


def dot(a, b, contract, precision=None):
    return lax.dot_general(
        a, b, ((contract[:1], contract[1:]), ((), ())), precision=precision, preferred_element_type=F32
    )


def place(head):
    return 2 * (head // 4) + head % 2, (head // 2) % 2


def map_row(bit, m, owner):
    return ((bit * 2 + m) * 8 + owner) * 16


def causal_mask(length):
    t = lax.broadcasted_iota(jnp.int32, (length, length), 0)
    s = lax.broadcasted_iota(jnp.int32, (length, length), 1)
    return t >= s


def running_columns(gates):
    lower = jnp.where(causal_mask(gates.shape[1]), 1.0, 0.0).astype(F32)
    return dot(lower, gates, (1, 1), lax.Precision.HIGHEST)


def running_rows(gates):
    lower = jnp.where(causal_mask(gates.shape[1]), 1.0, 0.0).astype(F32)
    return dot(gates, lower, (1, 1), lax.Precision.HIGHEST)


def products_kernel(q_ref, k_ref, v_ref, g_ref, gates_ref, out_ref):
    length = q_ref.shape[0]
    width = q_ref.shape[1] // GROUP
    columns = running_columns(gates_ref[...])
    for j in range(GROUP):
        lanes = slice(j * width, (j + 1) * width)
        owner, bit = place(j)
        run = columns[:, j : j + 1]
        closing = run[length - 1 : length]
        g_start = (g_ref[:, lanes].astype(F32) * jnp.exp(run)).astype(BF16)
        v_end = (v_ref[:, lanes].astype(F32) * jnp.exp(closing - run)).astype(BF16)
        to = 2 * owner + bit
        out_ref[to, 0:width] = dot(q_ref[:, lanes], g_start, (0, 0)).astype(BF16)
        out_ref[to, width : 2 * width] = dot(k_ref[:, lanes], v_end, (0, 0)).astype(BF16)
        out_ref[to, 2 * width :] = jnp.broadcast_to(closing, (PAD, width)).astype(BF16)


def inside_kernel(
    key_scale, map_scale, q_ref, k_ref, v_ref, g_ref, gates_ref, mq_ref, mk_ref, fk_ref, qb_ref, kb_ref, vg_ref, out_ref
):
    heads, width = mq_ref.shape[0], mq_ref.shape[1]
    causal = causal_mask(q_ref.shape[0])
    columns = running_columns(gates_ref[...])
    rows = running_rows(gates_ref[...])
    for j in range(heads):
        lanes = slice(j * width, (j + 1) * width)
        owner, bit = place(j)
        within = jnp.exp(jnp.where(causal, columns[:, j : j + 1] - rows[j : j + 1], -1e30))
        q, k, v, g = q_ref[:, lanes], k_ref[:, lanes], v_ref[:, lanes], g_ref[:, lanes]
        fq = dot(q, mq_ref[j], (1, 0)).astype(BF16)
        fk = (dot(k, mk_ref[j], (1, 0)) * key_scale).astype(BF16)
        scores = (dot(fq, fk, (1, 1)) * within).astype(BF16)
        grad_scores = (dot(g, v, (1, 1)) * within).astype(BF16)
        query_back = dot(grad_scores, fk, (1, 0))
        key_back = dot(grad_scores, fq, (0, 0)) * key_scale
        fk_ref[:, lanes] = fk
        qb_ref[:, lanes] = query_back
        kb_ref[:, lanes] = key_back
        vg_ref[:, lanes] = dot(scores, g, (0, 0))
        for m, (x, back) in enumerate(((q, query_back), (k, key_back))):
            part = dot(x, back.astype(BF16), (0, 0)) * map_scale
            at = map_row(bit, m, owner)
            for b in range(width // 8):
                to = at + (b // 8) * 8
                out_ref[b % 8, to : to + 8] = part[8 * b : 8 * b + 8].astype(BF16)


def over(decay, value):
    rows, width = value.shape
    return (decay[None] * value.reshape(rows // PAD, PAD, width)).reshape(rows, width)


def totals_kernel(key_scale, in_ref, mq_ref, mk_ref, blocks_ref, out_ref):
    near, heads, width = in_ref.shape[0], in_ref.shape[1], in_ref.shape[3]
    mine = lax.axis_index("outer")
    pair = lax.axis_index("inner") * 2 + lax.axis_index("x") // 2
    first = pair * 4 + lax.axis_index("x") % 2
    for h in range(heads):
        mq, mk = mq_ref[first + 2 * h], mk_ref[first + 2 * h]
        ahead = jnp.zeros((width, width), F32)
        back = jnp.zeros((width, width), F32)
        log = jnp.zeros((PAD, width), F32)
        for r in range(near):
            b = near - 1 - r
            state = dot(mk, in_ref[r, h, width : 2 * width], (0, 0)) * key_scale
            grad = dot(mq, in_ref[b, h, 0:width], (0, 0))
            blocks_ref[r, h, 0:width] = state.astype(BF16)
            blocks_ref[b, h, width:] = grad.astype(BF16)
            ahead = over(jnp.exp(in_ref[r, h, 2 * width :].astype(F32)), ahead) + state
            back = over(jnp.exp(in_ref[b, h, 2 * width :].astype(F32)), back) + grad
            log = log + in_ref[r, h, 2 * width :].astype(F32)
        coarse = log.astype(BF16)
        fine = (log - coarse.astype(F32)).astype(BF16)
        for o in range(out_ref.shape[0]):
            out_ref[o, h, 0:width] = jnp.where(o > mine, ahead, back).astype(BF16)
            out_ref[o, h, width : width + PAD] = coarse
            out_ref[o, h, width + PAD :] = fine


def spread_kernel(
    key_scale, map_scale, in_ref, blocks_ref, totals_ref, inside_ref, out_ref, states_ref, maps_ref, sems
):
    near, heads, width = in_ref.shape[0], in_ref.shape[1], in_ref.shape[3]
    groups = totals_ref.shape[0]
    mine = lax.axis_index("outer")

    def total(o, h):
        log = totals_ref[o, h, width : width + PAD].astype(F32) + totals_ref[o, h, width + PAD :].astype(F32)
        return jnp.exp(log), totals_ref[o, h, 0:width].astype(F32)

    for h in range(heads):
        ahead = jnp.zeros((width, width), F32)
        back = jnp.zeros((width, width), F32)
        for o in range(groups):
            decay, value = total(o, h)
            ahead = jnp.where(o < mine, over(decay, ahead) + value, ahead)
            b = groups - 1 - o
            decay, value = total(b, h)
            back = jnp.where(b > mine, over(decay, back) + value, back)
        sums = [jnp.zeros((width, width), F32), jnp.zeros((width, width), F32)]
        for r in range(near):
            b = near - 1 - r
            state_in, grad_in = ahead.astype(BF16), back.astype(BF16)
            states_ref[r, 2 * h * width : (2 * h + 1) * width] = state_in
            states_ref[b, (2 * h + 1) * width : (2 * h + 2) * width] = grad_in
            sums[0] = sums[0] + dot(in_ref[r, h, 0:width], state_in, (1, 1))
            sums[1] = sums[1] + dot(in_ref[b, h, width : 2 * width], grad_in, (1, 1))
            if r < near - 1:
                ahead = over(jnp.exp(in_ref[r, h, 2 * width :].astype(F32)), ahead) + blocks_ref[
                    r, h, 0:width
                ].astype(F32)
                back = over(jnp.exp(in_ref[b, h, 2 * width :].astype(F32)), back) + blocks_ref[b, h, width:].astype(F32)
        for m, scale in enumerate((map_scale, map_scale * key_scale)):
            part = sums[m] * scale
            for b in range(width // 8):
                to = ((h * 2 + m) * 2 + b // 8) * 8
                maps_ref[b % 8, to : to + 8] = part[8 * b : 8 * b + 8].astype(BF16)
    rows = 2 * heads * width
    start = rows + inside_rows(heads * near)
    copies = [
        pltpu.make_async_copy(states_ref, out_ref.at[:, 0:rows], sems.at[0]),
        pltpu.make_async_copy(maps_ref, out_ref.at[:, start : start + maps_ref.shape[1]], sems.at[1]),
    ]
    for copy in copies:
        copy.start()
    for copy in copies:
        copy.wait()


def inside_rows(heads):
    return heads * 2 * 16


def gather_kernel(inside_ref, carried_ref, out_ref):
    total = jnp.sum(inside_ref[...].astype(F32), axis=0)
    for r in range(inside_ref.shape[0]):
        for bit in range(2):
            for m in range(2):
                at, of = map_row(bit, m, r), (bit * 2 + m) * 16
                add = carried_ref[r, of : of + 16].astype(F32)
                out_ref[at : at + 16] = (total[at : at + 16] + add).astype(BF16)


def grads_kernel(
    key_scale, v_ref, g_ref, fk_ref, gates_ref, mq_ref, mk_ref, qb_ref, kb_ref, vgi_ref, in_ref, qg_ref, kg_ref, vg_ref
):
    width = mq_ref.shape[1]
    length = fk_ref.shape[0]
    columns = running_columns(gates_ref[...])
    for j in range(GROUP):
        lanes = slice(j * width, (j + 1) * width)
        owner, bit = place(j)
        run = columns[:, j : j + 1]
        start = jnp.exp(run)
        end = jnp.exp(run[length - 1 : length] - run)
        state_in = in_ref[owner, 2 * bit * width : (2 * bit + 1) * width]
        grad_in = in_ref[owner, (2 * bit + 1) * width : (2 * bit + 2) * width]
        query_back = (qb_ref[:, lanes] + dot(g_ref[:, lanes], state_in, (1, 1)) * start).astype(BF16)
        key_back = (kb_ref[:, lanes] + dot(v_ref[:, lanes], grad_in, (1, 1)) * (end * key_scale)).astype(BF16)
        vg_ref[:, lanes] = (vgi_ref[:, lanes] + dot(fk_ref[:, lanes], grad_in, (1, 0)) * end).astype(BF16)
        qg_ref[:, lanes] = dot(query_back, mq_ref[j], (1, 1)).astype(BF16)
        kg_ref[:, lanes] = dot(key_back, mk_ref[j], (1, 1)).astype(BF16)


def sum_kernel(in_ref, out_ref):
    out_ref[...] = jnp.sum(in_ref[...].astype(F32), axis=0).astype(out_ref.dtype)


def add_up(value, dtype):
    out_shape = jax.ShapeDtypeStruct(value.shape[1:], dtype)
    return pl.pallas_call(sum_kernel, out_shape=out_shape, compiler_params=VMEM)(value)


def exchange(value, axes):
    return lax.all_to_all(value, axes, 0, 0, tiled=True)


def per_device(queries, keys, values, out_grad, log_gates, query_map, key_map):
    heads, width = query_map.shape[0], query_map.shape[1]
    length = queries.shape[1]
    near, outer = lax.axis_size(NEAR), lax.axis_size("outer")
    key_scale = width ** (-0.5) / 16.0
    map_scale = (lax.axis_size(DP) * lax.axis_size(CONTEXT) * length) ** (-0.5)
    steps = heads // GROUP
    share = heads // near
    q, k, v, g = (x.reshape(length, heads * width) for x in (queries, keys, values, out_grad))
    gates = log_gates.reshape(heads, length)
    wide = pl.BlockSpec((length, GROUP * width), lambda i: (0, i))
    gate_spec = pl.BlockSpec((GROUP, length), lambda i: (i, 0))
    map_spec = pl.BlockSpec((GROUP, width, width), lambda i: (i, 0, 0))
    wide_shape = jax.ShapeDtypeStruct((length, heads * width), BF16)
    sum_shape = jax.ShapeDtypeStruct((length, heads * width), F32)
    flops = 2 * length * width * width * heads
    sent = pl.pallas_call(
        products_kernel,
        grid=(steps,),
        in_specs=[wide, wide, wide, wide, gate_spec],
        out_specs=pl.BlockSpec((GROUP, 2 * width + PAD, width), lambda i: (i, 0, 0)),
        out_shape=jax.ShapeDtypeStruct((heads, 2 * width + PAD, width), BF16),
        cost_estimate=pl.CostEstimate(flops=2 * flops, bytes_accessed=3 << 20, transcendentals=0),
    )(q, k, v, g, gates)
    received = exchange(sent.reshape(near, share, 2 * width + PAD, width), NEAR)
    rows = 2 * share * width
    payload = jax.ShapeDtypeStruct((near, rows + inside_rows(heads) + inside_rows(share), width), BF16)
    full = pl.BlockSpec((length, heads * width), lambda i: (0, 0))
    fk, query_inside, key_inside, value_inside, inside = pl.pallas_call(
        functools.partial(inside_kernel, key_scale, map_scale),
        grid=(1,),
        in_specs=[full] * 4
        + [pl.BlockSpec((heads, length), lambda i: (0, 0))]
        + [pl.BlockSpec((heads, width, width), lambda i: (0, 0, 0))] * 2,
        out_specs=[full] * 4 + [pl.BlockSpec((near, inside_rows(heads), width), lambda i: (0, 1, 0))],
        out_shape=[wide_shape] + [sum_shape] * 3 + [payload],
        cost_estimate=pl.CostEstimate(flops=9 * flops, bytes_accessed=8 << 20, transcendentals=1 << 18),
    )(q, k, v, g, gates, query_map, key_map)
    blocks, totals = pl.pallas_call(
        functools.partial(totals_kernel, key_scale),
        out_shape=[
            jax.ShapeDtypeStruct((near, share, 2 * width, width), BF16),
            jax.ShapeDtypeStruct((outer, share, width + 2 * PAD, width), BF16),
        ],
    )(received, query_map, key_map)
    totals = exchange(totals, "outer")
    whole = pl.BlockSpec(memory_space=pltpu.VMEM)
    spread = pl.pallas_call(
        functools.partial(spread_kernel, key_scale, map_scale),
        in_specs=[whole, whole, whole, pl.BlockSpec(memory_space=pl.ANY)],
        out_specs=pl.BlockSpec(memory_space=pl.ANY),
        out_shape=payload,
        scratch_shapes=[
            pltpu.VMEM((near, rows, width), BF16),
            pltpu.VMEM((near, inside_rows(share), width), BF16),
            pltpu.SemaphoreType.DMA((2,)),
        ],
        input_output_aliases={3: 0},
    )(received, blocks, totals, inside)
    carried = exchange(spread, NEAR)
    tail = (rows + inside_rows(heads)) // inside_rows(share)
    maps = pl.pallas_call(
        gather_kernel,
        grid=(1,),
        in_specs=[
            pl.BlockSpec((near, inside_rows(heads), width), lambda i: (0, 1, 0)),
            pl.BlockSpec((near, inside_rows(share), width), lambda i: (0, tail, 0)),
        ],
        out_specs=pl.BlockSpec((inside_rows(heads), width), lambda i: (0, 0)),
        out_shape=jax.ShapeDtypeStruct((inside_rows(heads), width), BF16),
    )(carried, carried)
    maps = exchange(maps.reshape(2, inside_rows(heads) // 2, width), "core")
    maps = exchange(add_up(maps, BF16).reshape(32, 8, width), ("y", "outer"))
    query_grad, key_grad, value_grad = pl.pallas_call(
        functools.partial(grads_kernel, key_scale),
        grid=(steps,),
        in_specs=[wide] * 3 + [gate_spec, map_spec, map_spec] + [wide] * 3
        + [pl.BlockSpec((near // steps, rows, width), lambda i: (i, 0, 0))],
        out_specs=[wide] * 3,
        out_shape=[wide_shape] * 3,
        cost_estimate=pl.CostEstimate(flops=5 * flops, bytes_accessed=8 << 20, transcendentals=0),
    )(v, g, fk, gates, query_map, key_map, query_inside, key_inside, value_inside, carried)
    map_grads = add_up(maps, F32)
    shape = queries.shape
    return query_grad.reshape(shape), key_grad.reshape(shape), value_grad.reshape(shape), map_grads


def solution(mesh):
    fine = Mesh(np.asarray(mesh.devices).reshape(8, 2, 4, 2, 4), DP + CONTEXT)
    split = P(DP, CONTEXT, None)
    return jax.shard_map(
        per_device,
        mesh=fine,
        in_specs=(split, split, split, split, P(DP, None, CONTEXT), P(), P()),
        out_specs=(split, split, split, P(DP + CONTEXT, None)),
        check_vma=False,
    )
```

```python
import functools

import jax
import jax.numpy as jnp
import numpy as np
from jax import lax
from jax.experimental import pallas as pl
from jax.experimental.pallas import tpu as pltpu
from jax.sharding import Mesh, PartitionSpec as P

F32 = jnp.float32
BF16 = jnp.bfloat16
GROUP = 8
PAD = 8
DP = ("y_hi", "y_lo", "core")
CONTEXT = ("outer", "inner", "x")
NEAR = ("inner", "x")
VMEM = pltpu.CompilerParams(vmem_limit_bytes=20 << 20)


def dot(a, b, contract, precision=None):
    return lax.dot_general(
        a, b, ((contract[:1], contract[1:]), ((), ())), precision=precision, preferred_element_type=F32
    )


def place(head):
    return 2 * (head // 4) + head % 2, (head // 2) % 2


def causal_mask(length):
    t = lax.broadcasted_iota(jnp.int32, (length, length), 0)
    s = lax.broadcasted_iota(jnp.int32, (length, length), 1)
    return t >= s


def running_columns(gates):
    lower = jnp.where(causal_mask(gates.shape[1]), 1.0, 0.0).astype(F32)
    return dot(lower, gates, (1, 1), lax.Precision.HIGHEST)


def running_rows(gates):
    lower = jnp.where(causal_mask(gates.shape[1]), 1.0, 0.0).astype(F32)
    return dot(gates, lower, (1, 1), lax.Precision.HIGHEST)


def products_kernel(q_ref, k_ref, v_ref, g_ref, gates_ref, out_ref):
    length = q_ref.shape[0]
    width = q_ref.shape[1] // GROUP
    columns = running_columns(gates_ref[...])
    for j in range(GROUP):
        lanes = slice(j * width, (j + 1) * width)
        owner, bit = place(j)
        run = columns[:, j : j + 1]
        closing = run[length - 1 : length]
        g_start = (g_ref[:, lanes].astype(F32) * jnp.exp(run)).astype(BF16)
        v_end = (v_ref[:, lanes].astype(F32) * jnp.exp(closing - run)).astype(BF16)
        to = 2 * owner + bit
        out_ref[to, 0:width] = dot(q_ref[:, lanes], g_start, (0, 0)).astype(BF16)
        out_ref[to, width : 2 * width] = dot(k_ref[:, lanes], v_end, (0, 0)).astype(BF16)
        out_ref[to, 2 * width :] = jnp.broadcast_to(closing, (PAD, width)).astype(BF16)


def inside_kernel(
    key_scale, map_scale, q_ref, k_ref, v_ref, g_ref, gates_ref, mq_ref, mk_ref, fk_ref, qb_ref, kb_ref, vg_ref, out_ref
):
    heads, width = mq_ref.shape[0], mq_ref.shape[1]
    core, y_lo = lax.axis_index("core"), lax.axis_index("y_lo")
    causal = causal_mask(q_ref.shape[0])
    columns = running_columns(gates_ref[...])
    rows = running_rows(gates_ref[...])
    for j in range(heads):
        lanes = slice(j * width, (j + 1) * width)
        owner, bit = place(j)
        side = 2 * lax.bitwise_xor(core, bit) + lax.bitwise_xor(y_lo, (owner // 2) % 2)
        within = jnp.exp(jnp.where(causal, columns[:, j : j + 1] - rows[j : j + 1], -1e30))
        q, k, v, g = q_ref[:, lanes], k_ref[:, lanes], v_ref[:, lanes], g_ref[:, lanes]
        fq = dot(q, mq_ref[j], (1, 0)).astype(BF16)
        fk = (dot(k, mk_ref[j], (1, 0)) * key_scale).astype(BF16)
        scores = (dot(fq, fk, (1, 1)) * within).astype(BF16)
        grad_scores = (dot(g, v, (1, 1)) * within).astype(BF16)
        query_back = dot(grad_scores, fk, (1, 0))
        key_back = dot(grad_scores, fq, (0, 0)) * key_scale
        fk_ref[:, lanes] = fk
        qb_ref[:, lanes] = query_back
        kb_ref[:, lanes] = key_back
        vg_ref[:, lanes] = dot(scores, g, (0, 0))
        for m, (x, back) in enumerate(((q, query_back), (k, key_back))):
            part = dot(x, back.astype(BF16), (0, 0)) * map_scale
            at = ((m * 2 + owner // 4) * 2 + owner % 2) * 16
            for b in range(width // 8):
                to = at + (b // 8) * 8
                out_ref[side, b % 8, to : to + 8] = part[8 * b : 8 * b + 8].astype(BF16)


def over(decay, value):
    rows, width = value.shape
    return (decay[None] * value.reshape(rows // PAD, PAD, width)).reshape(rows, width)


def totals_kernel(key_scale, in_ref, mq_ref, mk_ref, inside_ref, blocks_ref, out_ref):
    del inside_ref
    near, heads, width = in_ref.shape[0], in_ref.shape[1], in_ref.shape[3]
    mine = lax.axis_index("outer")
    pair = lax.axis_index("inner") * 2 + lax.axis_index("x") // 2
    first = pair * 4 + lax.axis_index("x") % 2
    for h in range(heads):
        mq, mk = mq_ref[first + 2 * h], mk_ref[first + 2 * h]
        ahead = jnp.zeros((width, width), F32)
        back = jnp.zeros((width, width), F32)
        log = jnp.zeros((PAD, width), F32)
        for r in range(near):
            b = near - 1 - r
            state = dot(mk, in_ref[r, h, width : 2 * width], (0, 0)) * key_scale
            grad = dot(mq, in_ref[b, h, 0:width], (0, 0))
            blocks_ref[r, h, 0:width] = state.astype(BF16)
            blocks_ref[b, h, width:] = grad.astype(BF16)
            ahead = over(jnp.exp(in_ref[r, h, 2 * width :].astype(F32)), ahead) + state
            back = over(jnp.exp(in_ref[b, h, 2 * width :].astype(F32)), back) + grad
            log = log + in_ref[r, h, 2 * width :].astype(F32)
        coarse = log.astype(BF16)
        fine = (log - coarse.astype(F32)).astype(BF16)
        for o in range(out_ref.shape[0]):
            out_ref[o, h, 0:width] = jnp.where(o > mine, ahead, back).astype(BF16)
            out_ref[o, h, width : width + PAD] = coarse
            out_ref[o, h, width + PAD :] = fine


def spread_kernel(
    key_scale, map_scale, in_ref, blocks_ref, totals_ref, inside_ref, out_ref, states_ref, maps_ref, sems
):
    near, heads, width = in_ref.shape[0], in_ref.shape[1], in_ref.shape[3]
    groups = totals_ref.shape[0]
    mine = lax.axis_index("outer")

    def total(o, h):
        log = totals_ref[o, h, width : width + PAD].astype(F32) + totals_ref[o, h, width + PAD :].astype(F32)
        return jnp.exp(log), totals_ref[o, h, 0:width].astype(F32)

    for h in range(heads):
        ahead = jnp.zeros((width, width), F32)
        back = jnp.zeros((width, width), F32)
        for o in range(groups):
            decay, value = total(o, h)
            ahead = jnp.where(o < mine, over(decay, ahead) + value, ahead)
            b = groups - 1 - o
            decay, value = total(b, h)
            back = jnp.where(b > mine, over(decay, back) + value, back)
        sums = [jnp.zeros((width, width), F32), jnp.zeros((width, width), F32)]
        for r in range(near):
            b = near - 1 - r
            state_in, grad_in = ahead.astype(BF16), back.astype(BF16)
            states_ref[r, 2 * h * width : (2 * h + 1) * width] = state_in
            states_ref[b, (2 * h + 1) * width : (2 * h + 2) * width] = grad_in
            sums[0] = sums[0] + dot(in_ref[r, h, 0:width], state_in, (1, 1))
            sums[1] = sums[1] + dot(in_ref[b, h, width : 2 * width], grad_in, (1, 1))
            if r < near - 1:
                ahead = over(jnp.exp(in_ref[r, h, 2 * width :].astype(F32)), ahead) + blocks_ref[
                    r, h, 0:width
                ].astype(F32)
                back = over(jnp.exp(in_ref[b, h, 2 * width :].astype(F32)), back) + blocks_ref[b, h, width:].astype(F32)
        for m, scale in enumerate((map_scale, map_scale * key_scale)):
            part = sums[m] * scale
            for b in range(width // 8):
                to = ((h * 2 + m) * 2 + b // 8) * 8
                maps_ref[b % 8, to : to + 8] = part[8 * b : 8 * b + 8].astype(BF16)
    rows = 2 * heads * width
    start = rows + inside_rows(heads * near) // 4
    copies = [
        pltpu.make_async_copy(states_ref, out_ref.at[:, 0:rows], sems.at[0]),
        pltpu.make_async_copy(maps_ref, out_ref.at[:, start : start + maps_ref.shape[1]], sems.at[1]),
    ]
    for copy in copies:
        copy.start()
    for copy in copies:
        copy.wait()


def inside_rows(heads):
    return heads * 2 * 16


def halve_kernel(kept_ref, got_ref, keep_ref, send_ref):
    keep_ref[...] = (kept_ref[0].astype(F32) + got_ref[0].astype(F32)).astype(BF16)
    send_ref[...] = (kept_ref[1].astype(F32) + got_ref[1].astype(F32)).astype(BF16)


def pair_kernel(kept_ref, got_ref, out_ref):
    out_ref[...] = (kept_ref[...].astype(F32) + got_ref[...].astype(F32)).astype(BF16)


def gather_kernel(inside_ref, carried_ref, out_ref):
    core, y_lo = lax.axis_index("core"), lax.axis_index("y_lo")
    for r in range(carried_ref.shape[0]):
        for bit in range(2):
            for m in range(2):
                of, to = (bit * 2 + m) * 16, (r % 2) * 16
                out_ref[bit, m, r // 4, (r // 2) % 2, to : to + 16] = carried_ref[r, of : of + 16]
    total = jnp.sum(inside_ref[...].astype(F32), axis=0)
    for m in range(2):
        for high in range(2):
            at = (m * 2 + high) * 32
            here = out_ref[core, m, high, y_lo].astype(F32)
            out_ref[core, m, high, y_lo] = (here + total[at : at + 32]).astype(BF16)


def grads_kernel(
    key_scale, v_ref, g_ref, fk_ref, gates_ref, mq_ref, mk_ref, qb_ref, kb_ref, vgi_ref, in_ref, qg_ref, kg_ref, vg_ref
):
    width = mq_ref.shape[1]
    length = fk_ref.shape[0]
    columns = running_columns(gates_ref[...])
    for j in range(GROUP):
        lanes = slice(j * width, (j + 1) * width)
        owner, bit = place(j)
        run = columns[:, j : j + 1]
        start = jnp.exp(run)
        end = jnp.exp(run[length - 1 : length] - run)
        state_in = in_ref[owner, 2 * bit * width : (2 * bit + 1) * width]
        grad_in = in_ref[owner, (2 * bit + 1) * width : (2 * bit + 2) * width]
        query_back = (qb_ref[:, lanes] + dot(g_ref[:, lanes], state_in, (1, 1)) * start).astype(BF16)
        key_back = (kb_ref[:, lanes] + dot(v_ref[:, lanes], grad_in, (1, 1)) * (end * key_scale)).astype(BF16)
        vg_ref[:, lanes] = (vgi_ref[:, lanes] + dot(fk_ref[:, lanes], grad_in, (1, 0)) * end).astype(BF16)
        qg_ref[:, lanes] = dot(query_back, mq_ref[j], (1, 1)).astype(BF16)
        kg_ref[:, lanes] = dot(key_back, mk_ref[j], (1, 1)).astype(BF16)


def sum_kernel(in_ref, out_ref):
    out_ref[...] = jnp.sum(in_ref[...].astype(F32), axis=0).astype(out_ref.dtype)


def add_up(value, dtype):
    out_shape = jax.ShapeDtypeStruct(value.shape[1:], dtype)
    return pl.pallas_call(sum_kernel, out_shape=out_shape, compiler_params=VMEM)(value)


def exchange(value, axes):
    return lax.all_to_all(value, axes, 0, 0, tiled=True)


def per_device(queries, keys, values, out_grad, log_gates, query_map, key_map):
    heads, width = query_map.shape[0], query_map.shape[1]
    length = queries.shape[1]
    near, outer = lax.axis_size(NEAR), lax.axis_size("outer")
    key_scale = width ** (-0.5) / 16.0
    map_scale = (lax.axis_size(DP) * lax.axis_size(CONTEXT) * length) ** (-0.5)
    steps = heads // GROUP
    share = heads // near
    q, k, v, g = (x.reshape(length, heads * width) for x in (queries, keys, values, out_grad))
    gates = log_gates.reshape(heads, length)
    wide = pl.BlockSpec((length, GROUP * width), lambda i: (0, i))
    gate_spec = pl.BlockSpec((GROUP, length), lambda i: (i, 0))
    map_spec = pl.BlockSpec((GROUP, width, width), lambda i: (i, 0, 0))
    wide_shape = jax.ShapeDtypeStruct((length, heads * width), BF16)
    sum_shape = jax.ShapeDtypeStruct((length, heads * width), F32)
    flops = 2 * length * width * width * heads
    sent = pl.pallas_call(
        products_kernel,
        grid=(steps,),
        in_specs=[wide, wide, wide, wide, gate_spec],
        out_specs=pl.BlockSpec((GROUP, 2 * width + PAD, width), lambda i: (i, 0, 0)),
        out_shape=jax.ShapeDtypeStruct((heads, 2 * width + PAD, width), BF16),
        cost_estimate=pl.CostEstimate(flops=2 * flops, bytes_accessed=3 << 20, transcendentals=0),
    )(q, k, v, g, gates)
    received = exchange(sent.reshape(near, share, 2 * width + PAD, width), NEAR)
    rows, quarter = 2 * share * width, inside_rows(heads) // 4
    full = pl.BlockSpec((length, heads * width), lambda i: (0, 0))
    fk, query_inside, key_inside, value_inside, inside = pl.pallas_call(
        functools.partial(inside_kernel, key_scale, map_scale),
        grid=(1,),
        in_specs=[full] * 4
        + [pl.BlockSpec((heads, length), lambda i: (0, 0))]
        + [pl.BlockSpec((heads, width, width), lambda i: (0, 0, 0))] * 2,
        out_specs=[full] * 4 + [pl.BlockSpec((4, near, quarter, width), lambda i: (0, 0, 0, 0))],
        out_shape=[wide_shape] + [sum_shape] * 3 + [jax.ShapeDtypeStruct((4, near, quarter, width), BF16)],
        cost_estimate=pl.CostEstimate(flops=9 * flops, bytes_accessed=8 << 20, transcendentals=1 << 18),
    )(q, k, v, g, gates, query_map, key_map)
    swap = [(0, 1), (1, 0)]
    got = lax.ppermute(inside[2:], "core", swap)
    part = jax.ShapeDtypeStruct((near, quarter, width), BF16)
    half = pl.BlockSpec((2, near, quarter, width), lambda i: (0, 0, 0, 0))
    whole_part = pl.BlockSpec((near, quarter, width), lambda i: (0, 0, 0))
    keep, send = pl.pallas_call(
        halve_kernel,
        grid=(1,),
        in_specs=[half, half],
        out_specs=[whole_part] * 2,
        out_shape=[part, part],
        compiler_params=VMEM,
    )(inside, got)
    got = lax.ppermute(send, "y_lo", swap)
    payload = jax.ShapeDtypeStruct((near, rows + quarter + inside_rows(share), width), BF16)
    mixed = pl.pallas_call(
        pair_kernel,
        grid=(1,),
        in_specs=[whole_part] * 2,
        out_specs=pl.BlockSpec((near, quarter, width), lambda i: (0, rows // quarter, 0)),
        out_shape=payload,
        compiler_params=VMEM,
    )(keep, got)
    whole = pl.BlockSpec(memory_space=pltpu.VMEM)
    blocks, totals = pl.pallas_call(
        functools.partial(totals_kernel, key_scale),
        in_specs=[whole] * 3 + [pl.BlockSpec(memory_space=pl.ANY)],
        out_shape=[
            jax.ShapeDtypeStruct((near, share, 2 * width, width), BF16),
            jax.ShapeDtypeStruct((outer, share, width + 2 * PAD, width), BF16),
        ],
    )(received, query_map, key_map, inside)
    totals = exchange(totals, "outer")
    spread = pl.pallas_call(
        functools.partial(spread_kernel, key_scale, map_scale),
        in_specs=[whole, whole, whole, pl.BlockSpec(memory_space=pl.ANY)],
        out_specs=pl.BlockSpec(memory_space=pl.ANY),
        out_shape=payload,
        scratch_shapes=[
            pltpu.VMEM((near, rows, width), BF16),
            pltpu.VMEM((near, inside_rows(share), width), BF16),
            pltpu.SemaphoreType.DMA((2,)),
        ],
        input_output_aliases={3: 0},
        compiler_params=VMEM,
    )(received, blocks, totals, mixed)
    carried = exchange(spread, NEAR)
    tail = (rows + quarter) // inside_rows(share)
    maps = pl.pallas_call(
        gather_kernel,
        grid=(1,),
        in_specs=[
            pl.BlockSpec((near, quarter, width), lambda i: (0, rows // quarter, 0)),
            pl.BlockSpec((near, inside_rows(share), width), lambda i: (0, tail, 0)),
        ],
        out_specs=pl.BlockSpec((2, 2, 2, 2, 32, width), lambda i: (0, 0, 0, 0, 0, 0)),
        out_shape=jax.ShapeDtypeStruct((2, 2, 2, 2, 32, width), BF16),
        compiler_params=VMEM,
    )(carried, carried)
    maps = exchange(maps.reshape(2, inside_rows(heads) // 2, width), "core")
    maps = exchange(add_up(maps, BF16).reshape(32, 8, width), ("y_hi", "y_lo", "outer"))
    query_grad, key_grad, value_grad = pl.pallas_call(
        functools.partial(grads_kernel, key_scale),
        grid=(steps,),
        in_specs=[wide] * 3 + [gate_spec, map_spec, map_spec] + [wide] * 3
        + [pl.BlockSpec((near // steps, rows, width), lambda i: (i, 0, 0))],
        out_specs=[wide] * 3,
        out_shape=[wide_shape] * 3,
        cost_estimate=pl.CostEstimate(flops=5 * flops, bytes_accessed=8 << 20, transcendentals=0),
    )(v, g, fk, gates, query_map, key_map, query_inside, key_inside, value_inside, carried)
    map_grads = add_up(maps, F32)
    shape = queries.shape
    return query_grad.reshape(shape), key_grad.reshape(shape), value_grad.reshape(shape), map_grads


def solution(mesh):
    fine = Mesh(np.asarray(mesh.devices).reshape(4, 2, 2, 4, 2, 4), DP + CONTEXT)
    split = P(DP, CONTEXT, None)
    return jax.shard_map(
        per_device,
        mesh=fine,
        in_specs=(split, split, split, split, P(DP, None, CONTEXT), P(), P()),
        out_specs=(split, split, split, P(DP + CONTEXT, None)),
        check_vma=False,
    )
```

```python
import functools

import jax
import jax.numpy as jnp
import numpy as np
from jax import lax
from jax.experimental import pallas as pl
from jax.experimental.pallas import tpu as pltpu
from jax.sharding import Mesh, PartitionSpec as P

F32 = jnp.float32
BF16 = jnp.bfloat16
GROUP = 8
PAD = 8
DP = ("y_hi", "y_lo", "core")
CONTEXT = ("outer", "inner", "x")
NEAR = ("inner", "x")
VMEM = pltpu.CompilerParams(vmem_limit_bytes=20 << 20)


def dot(a, b, contract, precision=None):
    return lax.dot_general(
        a, b, ((contract[:1], contract[1:]), ((), ())), precision=precision, preferred_element_type=F32
    )


def place(head):
    return 2 * (head // 4) + head % 2, (head // 2) % 2


def causal_mask(length):
    t = lax.broadcasted_iota(jnp.int32, (length, length), 0)
    s = lax.broadcasted_iota(jnp.int32, (length, length), 1)
    return t >= s


def running_columns(gates):
    lower = jnp.where(causal_mask(gates.shape[1]), 1.0, 0.0).astype(F32)
    return dot(lower, gates, (1, 1), lax.Precision.HIGHEST)


def running_rows(gates):
    lower = jnp.where(causal_mask(gates.shape[1]), 1.0, 0.0).astype(F32)
    return dot(gates, lower, (1, 1), lax.Precision.HIGHEST)


def products_kernel(q_ref, k_ref, v_ref, g_ref, gates_ref, out_ref):
    length = q_ref.shape[0]
    width = q_ref.shape[1] // GROUP
    columns = running_columns(gates_ref[...])
    for j in range(GROUP):
        lanes = slice(j * width, (j + 1) * width)
        owner, bit = place(j)
        run = columns[:, j : j + 1]
        closing = run[length - 1 : length]
        g_start = (g_ref[:, lanes].astype(F32) * jnp.exp(run)).astype(BF16)
        v_end = (v_ref[:, lanes].astype(F32) * jnp.exp(closing - run)).astype(BF16)
        to = 2 * owner + bit
        out_ref[to, 0:width] = dot(q_ref[:, lanes], g_start, (0, 0)).astype(BF16)
        out_ref[to, width : 2 * width] = dot(k_ref[:, lanes], v_end, (0, 0)).astype(BF16)
        out_ref[to, 2 * width :] = jnp.broadcast_to(closing, (PAD, width)).astype(BF16)


def owned_heads():
    x = lax.axis_index("x")
    return (lax.axis_index("inner") * 2 + x // 2) * 4 + x % 2


def inside_kernel(
    key_scale, map_scale, q_ref, k_ref, v_ref, g_ref, gates_ref, mq_ref, mk_ref,
    fq_ref, fk_ref, qb_ref, kb_ref, keep_ref, send_ref, own_ref,
):
    heads, width = mq_ref.shape[0], mq_ref.shape[1]
    core, y_lo = lax.axis_index("core"), lax.axis_index("y_lo")
    first = owned_heads()
    for bit in range(2):
        own_ref[0, bit] = mq_ref[first + 2 * bit]
        own_ref[1, bit] = mk_ref[first + 2 * bit]
    causal = causal_mask(q_ref.shape[0])
    columns = running_columns(gates_ref[...])
    rows = running_rows(gates_ref[...])
    for j in range(heads):
        lanes = slice(j * width, (j + 1) * width)
        owner, bit = place(j)
        within = jnp.exp(jnp.where(causal, columns[:, j : j + 1] - rows[j : j + 1], -1e30))
        q, k, v, g = q_ref[:, lanes], k_ref[:, lanes], v_ref[:, lanes], g_ref[:, lanes]
        fq = dot(q, mq_ref[j], (1, 0)).astype(BF16)
        fk = (dot(k, mk_ref[j], (1, 0)) * key_scale).astype(BF16)
        grad_scores = (dot(g, v, (1, 1)) * within).astype(BF16)
        query_back = dot(grad_scores, fk, (1, 0))
        key_back = dot(grad_scores, fq, (0, 0)) * key_scale
        fq_ref[:, lanes] = fq
        fk_ref[:, lanes] = fk
        qb_ref[:, lanes] = query_back
        kb_ref[:, lanes] = key_back
        parts = [dot(x, back.astype(BF16), (0, 0)) * map_scale for x, back in ((q, query_back), (k, key_back))]
        side = lax.bitwise_xor(y_lo, (owner // 2) % 2)

        def store(ref, parts=parts, side=side, owner=owner):
            for m in range(2):
                at = ((m * 2 + owner // 4) * 2 + owner % 2) * 16
                for b in range(width // 8):
                    to = at + (b // 8) * 8
                    ref[side, b % 8, to : to + 8] = parts[m][8 * b : 8 * b + 8].astype(BF16)

        pl.when(core == bit)(functools.partial(store, keep_ref))
        pl.when(core != bit)(functools.partial(store, send_ref))


def over(decay, value):
    rows, width = value.shape
    return (decay[None] * value.reshape(rows // PAD, PAD, width)).reshape(rows, width)


def decay_of(ref, r, h, width):
    return jnp.exp(ref[r, h, 2 * width :].astype(F32))


def block_state(key_scale, in_ref, own_ref, r, h, width):
    return dot(own_ref[1, h], in_ref[r, h, width : 2 * width], (0, 0)) * key_scale


def block_grad(in_ref, own_ref, r, h, width):
    return dot(own_ref[0, h], in_ref[r, h, 0:width], (0, 0))


def totals_kernel(key_scale, in_ref, own_ref, out_ref):
    near, heads, width = in_ref.shape[0], in_ref.shape[1], in_ref.shape[3]
    mine = lax.axis_index("outer")
    for h in range(heads):
        ahead = jnp.zeros((width, width), F32)
        back = jnp.zeros((width, width), F32)
        log = jnp.zeros((PAD, width), F32)
        for r in range(near):
            b = near - 1 - r
            ahead = over(decay_of(in_ref, r, h, width), ahead) + block_state(key_scale, in_ref, own_ref, r, h, width)
            back = over(decay_of(in_ref, b, h, width), back) + block_grad(in_ref, own_ref, b, h, width)
            log = log + in_ref[r, h, 2 * width :].astype(F32)
        coarse = log.astype(BF16)
        fine = (log - coarse.astype(F32)).astype(BF16)
        for o in range(out_ref.shape[0]):
            out_ref[o, h, 0:width] = jnp.where(o > mine, ahead, back).astype(BF16)
            out_ref[o, h, width : width + PAD] = coarse
            out_ref[o, h, width + PAD :] = fine


def spread_kernel(
    key_scale, map_scale, in_ref, own_ref, totals_ref, inside_ref, out_ref, states_ref, maps_ref, sems
):
    near, heads, width = in_ref.shape[0], in_ref.shape[1], in_ref.shape[3]
    groups = totals_ref.shape[0]
    mine = lax.axis_index("outer")

    def total(o, h):
        log = totals_ref[o, h, width : width + PAD].astype(F32) + totals_ref[o, h, width + PAD :].astype(F32)
        return jnp.exp(log), totals_ref[o, h, 0:width].astype(F32)

    for h in range(heads):
        ahead = jnp.zeros((width, width), F32)
        back = jnp.zeros((width, width), F32)
        for o in range(groups):
            decay, value = total(o, h)
            ahead = jnp.where(o < mine, over(decay, ahead) + value, ahead)
            b = groups - 1 - o
            decay, value = total(b, h)
            back = jnp.where(b > mine, over(decay, back) + value, back)
        sums = [jnp.zeros((width, width), F32), jnp.zeros((width, width), F32)]
        for r in range(near):
            b = near - 1 - r
            state_in, grad_in = ahead.astype(BF16), back.astype(BF16)
            states_ref[r, 2 * h * width : (2 * h + 1) * width] = state_in
            states_ref[b, (2 * h + 1) * width : (2 * h + 2) * width] = grad_in
            sums[0] = sums[0] + dot(in_ref[r, h, 0:width], state_in, (1, 1))
            sums[1] = sums[1] + dot(in_ref[b, h, width : 2 * width], grad_in, (1, 1))
            if r < near - 1:
                state = block_state(key_scale, in_ref, own_ref, r, h, width)
                ahead = over(decay_of(in_ref, r, h, width), ahead) + state
                back = over(decay_of(in_ref, b, h, width), back) + block_grad(in_ref, own_ref, b, h, width)
        for m, scale in enumerate((map_scale, map_scale * key_scale)):
            part = sums[m] * scale
            for b in range(width // 8):
                to = ((h * 2 + m) * 2 + b // 8) * 8
                maps_ref[b % 8, to : to + 8] = part[8 * b : 8 * b + 8].astype(BF16)
    rows = 2 * heads * width
    start = rows + inside_rows(heads * near) // 4
    copies = [
        pltpu.make_async_copy(states_ref, out_ref.at[:, 0:rows], sems.at[0]),
        pltpu.make_async_copy(maps_ref, out_ref.at[:, start : start + maps_ref.shape[1]], sems.at[1]),
    ]
    for copy in copies:
        copy.start()
    for copy in copies:
        copy.wait()


def inside_rows(heads):
    return heads * 2 * 16


def halve_kernel(kept_ref, got_ref, keep_ref, send_ref):
    keep_ref[...] = (kept_ref[0].astype(F32) + got_ref[0].astype(F32)).astype(BF16)
    send_ref[...] = (kept_ref[1].astype(F32) + got_ref[1].astype(F32)).astype(BF16)


def pair_kernel(kept_ref, got_ref, out_ref):
    out_ref[...] = (kept_ref[...].astype(F32) + got_ref[...].astype(F32)).astype(BF16)


def gather_kernel(inside_ref, carried_ref, out_ref):
    core, y_lo = lax.axis_index("core"), lax.axis_index("y_lo")
    for r in range(carried_ref.shape[0]):
        for bit in range(2):
            for m in range(2):
                of, to = (bit * 2 + m) * 16, (r % 2) * 16
                out_ref[bit, m, r // 4, (r // 2) % 2, to : to + 16] = carried_ref[r, of : of + 16]
    total = jnp.sum(inside_ref[...].astype(F32), axis=0)
    for m in range(2):
        for high in range(2):
            at = (m * 2 + high) * 32
            here = out_ref[core, m, high, y_lo].astype(F32)
            out_ref[core, m, high, y_lo] = (here + total[at : at + 32]).astype(BF16)


def grads_kernel(
    key_scale, v_ref, g_ref, fq_ref, fk_ref, gates_ref, mq_ref, mk_ref, qb_ref, kb_ref, in_ref, qg_ref, kg_ref, vg_ref
):
    width = mq_ref.shape[1]
    length = fk_ref.shape[0]
    causal = causal_mask(length)
    columns = running_columns(gates_ref[...])
    rows = running_rows(gates_ref[...])
    for j in range(GROUP):
        lanes = slice(j * width, (j + 1) * width)
        owner, bit = place(j)
        run = columns[:, j : j + 1]
        within = jnp.exp(jnp.where(causal, run - rows[j : j + 1], -1e30))
        start = jnp.exp(run)
        end = jnp.exp(run[length - 1 : length] - run)
        state_in = in_ref[owner, 2 * bit * width : (2 * bit + 1) * width]
        grad_in = in_ref[owner, (2 * bit + 1) * width : (2 * bit + 2) * width]
        g, fk = g_ref[:, lanes], fk_ref[:, lanes]
        scores = (dot(fq_ref[:, lanes], fk, (1, 1)) * within).astype(BF16)
        query_back = (qb_ref[:, lanes] + dot(g, state_in, (1, 1)) * start).astype(BF16)
        key_back = (kb_ref[:, lanes] + dot(v_ref[:, lanes], grad_in, (1, 1)) * (end * key_scale)).astype(BF16)
        vg_ref[:, lanes] = (dot(scores, g, (0, 0)) + dot(fk, grad_in, (1, 0)) * end).astype(BF16)
        qg_ref[:, lanes] = dot(query_back, mq_ref[j], (1, 1)).astype(BF16)
        kg_ref[:, lanes] = dot(key_back, mk_ref[j], (1, 1)).astype(BF16)


def sum_kernel(in_ref, out_ref):
    out_ref[...] = jnp.sum(in_ref[...].astype(F32), axis=0).astype(out_ref.dtype)


def add_up(value, dtype):
    out_shape = jax.ShapeDtypeStruct(value.shape[1:], dtype)
    return pl.pallas_call(sum_kernel, out_shape=out_shape, compiler_params=VMEM)(value)


def exchange(value, axes):
    return lax.all_to_all(value, axes, 0, 0, tiled=True)


def per_device(queries, keys, values, out_grad, log_gates, query_map, key_map):
    heads, width = query_map.shape[0], query_map.shape[1]
    length = queries.shape[1]
    near, outer = lax.axis_size(NEAR), lax.axis_size("outer")
    key_scale = width ** (-0.5) / 16.0
    map_scale = (lax.axis_size(DP) * lax.axis_size(CONTEXT) * length) ** (-0.5)
    steps = heads // GROUP
    share = heads // near
    q, k, v, g = (x.reshape(length, heads * width) for x in (queries, keys, values, out_grad))
    gates = log_gates.reshape(heads, length)
    wide = pl.BlockSpec((length, GROUP * width), lambda i: (0, i))
    gate_spec = pl.BlockSpec((GROUP, length), lambda i: (i, 0))
    map_spec = pl.BlockSpec((GROUP, width, width), lambda i: (i, 0, 0))
    wide_shape = jax.ShapeDtypeStruct((length, heads * width), BF16)
    sum_shape = jax.ShapeDtypeStruct((length, heads * width), F32)
    flops = 2 * length * width * width * heads
    sent = pl.pallas_call(
        products_kernel,
        grid=(steps,),
        in_specs=[wide, wide, wide, wide, gate_spec],
        out_specs=pl.BlockSpec((GROUP, 2 * width + PAD, width), lambda i: (i, 0, 0)),
        out_shape=jax.ShapeDtypeStruct((heads, 2 * width + PAD, width), BF16),
        cost_estimate=pl.CostEstimate(flops=2 * flops, bytes_accessed=3 << 20, transcendentals=0),
    )(q, k, v, g, gates)
    received = exchange(sent.reshape(near, share, 2 * width + PAD, width), NEAR)
    rows, quarter = 2 * share * width, inside_rows(heads) // 4
    full = pl.BlockSpec((length, heads * width), lambda i: (0, 0))
    half = pl.BlockSpec((2, near, quarter, width), lambda i: (0, 0, 0, 0))
    half_shape = jax.ShapeDtypeStruct((2, near, quarter, width), BF16)
    fq, fk, query_inside, key_inside, keep, send, own = pl.pallas_call(
        functools.partial(inside_kernel, key_scale, map_scale),
        grid=(1,),
        in_specs=[full] * 4
        + [pl.BlockSpec((heads, length), lambda i: (0, 0))]
        + [pl.BlockSpec((heads, width, width), lambda i: (0, 0, 0))] * 2,
        out_specs=[full] * 4 + [half, half, pl.BlockSpec((2, share, width, width), lambda i: (0, 0, 0, 0))],
        out_shape=[wide_shape] * 2 + [sum_shape] * 2 + [half_shape] * 2
        + [jax.ShapeDtypeStruct((2, share, width, width), BF16)],
        cost_estimate=pl.CostEstimate(flops=7 * flops, bytes_accessed=8 << 20, transcendentals=1 << 18),
    )(q, k, v, g, gates, query_map, key_map)
    swap = [(0, 1), (1, 0)]
    got = lax.ppermute(send, "core", swap)
    part = jax.ShapeDtypeStruct((near, quarter, width), BF16)
    whole_part = pl.BlockSpec((near, quarter, width), lambda i: (0, 0, 0))
    keep, send = pl.pallas_call(
        halve_kernel,
        grid=(1,),
        in_specs=[half, half],
        out_specs=[whole_part] * 2,
        out_shape=[part, part],
        compiler_params=VMEM,
    )(keep, got)
    got = lax.ppermute(send, "y_lo", swap)
    payload = jax.ShapeDtypeStruct((near, rows + quarter + inside_rows(share), width), BF16)
    mixed = pl.pallas_call(
        pair_kernel,
        grid=(1,),
        in_specs=[whole_part] * 2,
        out_specs=pl.BlockSpec((near, quarter, width), lambda i: (0, rows // quarter, 0)),
        out_shape=payload,
        compiler_params=VMEM,
    )(keep, got)
    whole = pl.BlockSpec(memory_space=pltpu.VMEM)
    totals = pl.pallas_call(
        functools.partial(totals_kernel, key_scale),
        in_specs=[whole] * 2,
        out_shape=jax.ShapeDtypeStruct((outer, share, width + 2 * PAD, width), BF16),
        compiler_params=VMEM,
    )(received, own)
    totals = exchange(totals, "outer")
    spread = pl.pallas_call(
        functools.partial(spread_kernel, key_scale, map_scale),
        in_specs=[whole, whole, whole, pl.BlockSpec(memory_space=pl.ANY)],
        out_specs=pl.BlockSpec(memory_space=pl.ANY),
        out_shape=payload,
        scratch_shapes=[
            pltpu.VMEM((near, rows, width), BF16),
            pltpu.VMEM((near, inside_rows(share), width), BF16),
            pltpu.SemaphoreType.DMA((2,)),
        ],
        input_output_aliases={3: 0},
        compiler_params=VMEM,
    )(received, own, totals, mixed)
    carried = exchange(spread, NEAR)
    tail = (rows + quarter) // inside_rows(share)
    maps = pl.pallas_call(
        gather_kernel,
        grid=(1,),
        in_specs=[
            pl.BlockSpec((near, quarter, width), lambda i: (0, rows // quarter, 0)),
            pl.BlockSpec((near, inside_rows(share), width), lambda i: (0, tail, 0)),
        ],
        out_specs=pl.BlockSpec((2, 2, 2, 2, 32, width), lambda i: (0, 0, 0, 0, 0, 0)),
        out_shape=jax.ShapeDtypeStruct((2, 2, 2, 2, 32, width), BF16),
        compiler_params=VMEM,
    )(carried, carried)
    maps = exchange(maps.reshape(2, inside_rows(heads) // 2, width), "core")
    maps = exchange(add_up(maps, BF16).reshape(32, 8, width), ("y_hi", "y_lo", "outer"))
    query_grad, key_grad, value_grad = pl.pallas_call(
        functools.partial(grads_kernel, key_scale),
        grid=(steps,),
        in_specs=[wide] * 4 + [gate_spec, map_spec, map_spec] + [wide] * 2
        + [pl.BlockSpec((near // steps, rows, width), lambda i: (i, 0, 0))],
        out_specs=[wide] * 3,
        out_shape=[wide_shape] * 3,
        cost_estimate=pl.CostEstimate(flops=7 * flops, bytes_accessed=8 << 20, transcendentals=0),
    )(v, g, fq, fk, gates, query_map, key_map, query_inside, key_inside, carried)
    map_grads = add_up(maps, F32)
    shape = queries.shape
    return query_grad.reshape(shape), key_grad.reshape(shape), value_grad.reshape(shape), map_grads


def solution(mesh):
    fine = Mesh(np.asarray(mesh.devices).reshape(4, 2, 2, 4, 2, 4), DP + CONTEXT)
    split = P(DP, CONTEXT, None)
    return jax.shard_map(
        per_device,
        mesh=fine,
        in_specs=(split, split, split, split, P(DP, None, CONTEXT), P(), P()),
        out_specs=(split, split, split, P(DP + CONTEXT, None)),
        check_vma=False,
    )
```

```python
import functools

import jax
import jax.numpy as jnp
import numpy as np
from jax import lax
from jax.experimental import pallas as pl
from jax.experimental.pallas import tpu as pltpu
from jax.sharding import Mesh, PartitionSpec as P

F32 = jnp.float32
BF16 = jnp.bfloat16
GROUP = 8
PAD = 8
DP = ("y_hi", "y_lo", "core")
CONTEXT = ("outer", "inner", "x")
NEAR = ("inner", "x")
VMEM = pltpu.CompilerParams(vmem_limit_bytes=20 << 20)


def dot(a, b, contract, precision=None):
    return lax.dot_general(
        a, b, ((contract[:1], contract[1:]), ((), ())), precision=precision, preferred_element_type=F32
    )


def place(head):
    return 2 * (head // 4) + head % 2, (head // 2) % 2


def causal_mask(length):
    t = lax.broadcasted_iota(jnp.int32, (length, length), 0)
    s = lax.broadcasted_iota(jnp.int32, (length, length), 1)
    return t >= s


def running_columns(gates):
    lower = jnp.where(causal_mask(gates.shape[1]), 1.0, 0.0).astype(F32)
    return dot(lower, gates, (1, 1), lax.Precision.HIGHEST)


def running_rows(gates):
    lower = jnp.where(causal_mask(gates.shape[1]), 1.0, 0.0).astype(F32)
    return dot(gates, lower, (1, 1), lax.Precision.HIGHEST)


def products_kernel(q_ref, k_ref, v_ref, g_ref, gates_ref, out_ref):
    length = q_ref.shape[0]
    width = q_ref.shape[1] // GROUP
    columns = running_columns(gates_ref[...])
    for j in range(GROUP):
        lanes = slice(j * width, (j + 1) * width)
        owner, bit = place(j)
        run = columns[:, j : j + 1]
        closing = run[length - 1 : length]
        g_start = (g_ref[:, lanes].astype(F32) * jnp.exp(run)).astype(BF16)
        v_end = (v_ref[:, lanes].astype(F32) * jnp.exp(closing - run)).astype(BF16)
        to = 2 * owner + bit
        out_ref[to, 0:width] = dot(q_ref[:, lanes], g_start, (0, 0)).astype(BF16)
        out_ref[to, width : 2 * width] = dot(k_ref[:, lanes], v_end, (0, 0)).astype(BF16)
        out_ref[to, 2 * width :] = jnp.broadcast_to(closing, (PAD, width)).astype(BF16)


def owned_heads():
    x = lax.axis_index("x")
    return (lax.axis_index("inner") * 2 + x // 2) * 4 + x % 2


def inside_kernel(
    key_scale, map_scale, q_ref, k_ref, v_ref, g_ref, gates_ref, mq_ref, mk_ref,
    fq_ref, fk_ref, qb_ref, kb_ref, keep_ref, send_ref, maps_ref, sems,
):
    heads, width = mq_ref.shape[0], mq_ref.shape[1]
    causal = causal_mask(q_ref.shape[0])
    columns = running_columns(gates_ref[...])
    rows = running_rows(gates_ref[...])
    for j in range(heads):
        lanes = slice(j * width, (j + 1) * width)
        owner, bit = place(j)
        within = jnp.exp(jnp.where(causal, columns[:, j : j + 1] - rows[j : j + 1], -1e30))
        q, k, v, g = q_ref[:, lanes], k_ref[:, lanes], v_ref[:, lanes], g_ref[:, lanes]
        fq = dot(q, mq_ref[j], (1, 0)).astype(BF16)
        fk = (dot(k, mk_ref[j], (1, 0)) * key_scale).astype(BF16)
        grad_scores = (dot(g, v, (1, 1)) * within).astype(BF16)
        query_back = dot(grad_scores, fk, (1, 0))
        key_back = dot(grad_scores, fq, (0, 0)) * key_scale
        fq_ref[:, lanes] = fq
        fk_ref[:, lanes] = fk
        qb_ref[:, lanes] = query_back
        kb_ref[:, lanes] = key_back
        for m, (x, back) in enumerate(((q, query_back), (k, key_back))):
            part = dot(x, back.astype(BF16), (0, 0)) * map_scale
            at = ((m * 2 + owner // 4) * 2 + owner % 2) * 16
            for b in range(width // 8):
                to = at + (b // 8) * 8
                maps_ref[bit, (owner // 2) % 2, b % 8, to : to + 8] = part[8 * b : 8 * b + 8].astype(BF16)
    core, y_lo = lax.axis_index("core"), lax.axis_index("y_lo")
    copies = []
    for side in range(2):
        along = lax.bitwise_xor(y_lo, side)
        copies.append(pltpu.make_async_copy(maps_ref.at[core, along], keep_ref.at[side], sems.at[2 * side]))
        copies.append(pltpu.make_async_copy(maps_ref.at[1 - core, along], send_ref.at[side], sems.at[2 * side + 1]))
    for copy in copies:
        copy.start()
    for copy in copies:
        copy.wait()


def over(decay, value):
    rows, width = value.shape
    return (decay[None] * value.reshape(rows // PAD, PAD, width)).reshape(rows, width)


def decay_of(ref, r, h, width):
    return jnp.exp(ref[r, h, 2 * width :].astype(F32))


def block_state(key_scale, in_ref, map_ref, head, r, h, width):
    return dot(map_ref[head], in_ref[r, h, width : 2 * width], (0, 0)) * key_scale


def block_grad(in_ref, map_ref, head, r, h, width):
    return dot(map_ref[head], in_ref[r, h, 0:width], (0, 0))


def totals_kernel(key_scale, in_ref, mq_ref, mk_ref, out_ref):
    near, heads, width = in_ref.shape[0], in_ref.shape[1], in_ref.shape[3]
    mine = lax.axis_index("outer")
    for h in range(heads):
        head = owned_heads() + 2 * h
        ahead = jnp.zeros((width, width), F32)
        back = jnp.zeros((width, width), F32)
        log = jnp.zeros((PAD, width), F32)
        for r in range(near):
            b = near - 1 - r
            state = block_state(key_scale, in_ref, mk_ref, head, r, h, width)
            ahead = over(decay_of(in_ref, r, h, width), ahead) + state
            back = over(decay_of(in_ref, b, h, width), back) + block_grad(in_ref, mq_ref, head, b, h, width)
            log = log + in_ref[r, h, 2 * width :].astype(F32)
        coarse = log.astype(BF16)
        fine = (log - coarse.astype(F32)).astype(BF16)
        for o in range(out_ref.shape[0]):
            out_ref[o, h, 0:width] = jnp.where(o > mine, ahead, back).astype(BF16)
            out_ref[o, h, width : width + PAD] = coarse
            out_ref[o, h, width + PAD :] = fine


def blocks_kernel(key_scale, in_ref, mq_ref, mk_ref, out_ref):
    near, heads, width = in_ref.shape[0], in_ref.shape[1], in_ref.shape[3]
    for h in range(heads):
        head = owned_heads() + 2 * h
        for r in range(near):
            out_ref[r, h, 0:width] = block_state(key_scale, in_ref, mk_ref, head, r, h, width).astype(BF16)
            out_ref[r, h, width:] = block_grad(in_ref, mq_ref, head, r, h, width).astype(BF16)


def spread_kernel(key_scale, map_scale, in_ref, blocks_ref, totals_ref, states_ref, maps_ref):
    near, heads, width = in_ref.shape[0], in_ref.shape[1], in_ref.shape[3]
    groups = totals_ref.shape[0]
    mine, core = lax.axis_index("outer"), lax.axis_index("core")

    def total(o, h):
        log = totals_ref[o, h, width : width + PAD].astype(F32) + totals_ref[o, h, width + PAD :].astype(F32)
        return jnp.exp(log), totals_ref[o, h, 0:width].astype(F32)

    for h in range(heads):
        ahead = jnp.zeros((width, width), F32)
        back = jnp.zeros((width, width), F32)
        for o in range(groups):
            decay, value = total(o, h)
            ahead = jnp.where(o < mine, over(decay, ahead) + value, ahead)
            b = groups - 1 - o
            decay, value = total(b, h)
            back = jnp.where(b > mine, over(decay, back) + value, back)
        sums = [jnp.zeros((width, width), F32), jnp.zeros((width, width), F32)]
        for r in range(near):
            b = near - 1 - r
            state_in, grad_in = ahead.astype(BF16), back.astype(BF16)
            states_ref[r, 2 * h * width : (2 * h + 1) * width] = state_in
            states_ref[b, (2 * h + 1) * width : (2 * h + 2) * width] = grad_in
            sums[0] = sums[0] + dot(in_ref[r, h, 0:width], state_in, (1, 1))
            sums[1] = sums[1] + dot(in_ref[b, h, width : 2 * width], grad_in, (1, 1))
            if r < near - 1:
                ahead = over(decay_of(in_ref, r, h, width), ahead) + blocks_ref[r, h, 0:width].astype(F32)
                back = over(decay_of(in_ref, b, h, width), back) + blocks_ref[b, h, width:].astype(F32)
        side = lax.bitwise_xor(core, h)
        for m, scale in enumerate((map_scale, map_scale * key_scale)):
            part = sums[m] * scale
            for b in range(width // 8):
                to = (m * 2 + b // 8) * 8
                maps_ref[side, b % 8, to : to + 8] = part[8 * b : 8 * b + 8].astype(BF16)


def halve_kernel(kept_ref, got_ref, keep_ref, send_ref):
    keep_ref[...] = (kept_ref[0].astype(F32) + got_ref[0].astype(F32)).astype(BF16)
    send_ref[...] = (kept_ref[1].astype(F32) + got_ref[1].astype(F32)).astype(BF16)


def pair_kernel(inside_ref, inside_got_ref, carried_ref, carried_got_ref, out_ref):
    rows = inside_ref.shape[1]
    out_ref[:, 0:rows] = (inside_ref[...].astype(F32) + inside_got_ref[...].astype(F32)).astype(BF16)
    out_ref[:, rows:] = (carried_ref[0].astype(F32) + carried_got_ref[...].astype(F32)).astype(BF16)


def gather_kernel(in_ref, out_ref):
    y_lo = lax.axis_index("y_lo")
    rows = in_ref.shape[1] - 32
    for r in range(in_ref.shape[0]):
        for m in range(2):
            of, to = rows + m * 16, (r % 2) * 16
            out_ref[m, r // 4, (r // 2) % 2, to : to + 16] = in_ref[r, of : of + 16]
    total = jnp.sum(in_ref[:, 0:rows].astype(F32), axis=0)
    for m in range(2):
        for high in range(2):
            at = (m * 2 + high) * 32
            here = out_ref[m, high, y_lo].astype(F32)
            out_ref[m, high, y_lo] = (here + total[at : at + 32]).astype(BF16)


def grads_kernel(
    key_scale, v_ref, g_ref, fq_ref, fk_ref, gates_ref, mq_ref, mk_ref, qb_ref, kb_ref, in_ref, qg_ref, kg_ref, vg_ref
):
    width = mq_ref.shape[1]
    length = fk_ref.shape[0]
    causal = causal_mask(length)
    columns = running_columns(gates_ref[...])
    rows = running_rows(gates_ref[...])
    for j in range(GROUP):
        lanes = slice(j * width, (j + 1) * width)
        owner, bit = place(j)
        run = columns[:, j : j + 1]
        within = jnp.exp(jnp.where(causal, run - rows[j : j + 1], -1e30))
        start = jnp.exp(run)
        end = jnp.exp(run[length - 1 : length] - run)
        state_in = in_ref[owner, 2 * bit * width : (2 * bit + 1) * width]
        grad_in = in_ref[owner, (2 * bit + 1) * width : (2 * bit + 2) * width]
        g, fk = g_ref[:, lanes], fk_ref[:, lanes]
        scores = (dot(fq_ref[:, lanes], fk, (1, 1)) * within).astype(BF16)
        query_back = (qb_ref[:, lanes] + dot(g, state_in, (1, 1)) * start).astype(BF16)
        key_back = (kb_ref[:, lanes] + dot(v_ref[:, lanes], grad_in, (1, 1)) * (end * key_scale)).astype(BF16)
        vg_ref[:, lanes] = (dot(scores, g, (0, 0)) + dot(fk, grad_in, (1, 0)) * end).astype(BF16)
        qg_ref[:, lanes] = dot(query_back, mq_ref[j], (1, 1)).astype(BF16)
        kg_ref[:, lanes] = dot(key_back, mk_ref[j], (1, 1)).astype(BF16)


def sum_kernel(in_ref, out_ref):
    out_ref[...] = jnp.sum(in_ref[...].astype(F32), axis=0).astype(out_ref.dtype)


def add_up(value, dtype):
    out_shape = jax.ShapeDtypeStruct(value.shape[1:], dtype)
    return pl.pallas_call(sum_kernel, out_shape=out_shape, compiler_params=VMEM)(value)


def exchange(value, axes):
    return lax.all_to_all(value, axes, 0, 0, tiled=True)


def per_device(queries, keys, values, out_grad, log_gates, query_map, key_map):
    heads, width = query_map.shape[0], query_map.shape[1]
    length = queries.shape[1]
    near, outer = lax.axis_size(NEAR), lax.axis_size("outer")
    key_scale = width ** (-0.5) / 16.0
    map_scale = (lax.axis_size(DP) * lax.axis_size(CONTEXT) * length) ** (-0.5)
    steps = heads // GROUP
    share = heads // near
    q, k, v, g = (x.reshape(length, heads * width) for x in (queries, keys, values, out_grad))
    gates = log_gates.reshape(heads, length)
    wide = pl.BlockSpec((length, GROUP * width), lambda i: (0, i))
    gate_spec = pl.BlockSpec((GROUP, length), lambda i: (i, 0))
    map_spec = pl.BlockSpec((GROUP, width, width), lambda i: (i, 0, 0))
    wide_shape = jax.ShapeDtypeStruct((length, heads * width), BF16)
    sum_shape = jax.ShapeDtypeStruct((length, heads * width), F32)
    flops = 2 * length * width * width * heads
    sent = pl.pallas_call(
        products_kernel,
        grid=(steps,),
        in_specs=[wide, wide, wide, wide, gate_spec],
        out_specs=pl.BlockSpec((GROUP, 2 * width + PAD, width), lambda i: (i, 0, 0)),
        out_shape=jax.ShapeDtypeStruct((heads, 2 * width + PAD, width), BF16),
        cost_estimate=pl.CostEstimate(flops=2 * flops, bytes_accessed=3 << 20, transcendentals=0),
    )(q, k, v, g, gates)
    received = exchange(sent.reshape(near, share, 2 * width + PAD, width), NEAR)
    rows, quarter = 2 * share * width, heads * 8
    full = pl.BlockSpec((length, heads * width), lambda i: (0, 0))
    half_shape = jax.ShapeDtypeStruct((2, near, quarter, width), BF16)
    anywhere = pl.BlockSpec(memory_space=pl.ANY)
    fq, fk, query_inside, key_inside, keep, send = pl.pallas_call(
        functools.partial(inside_kernel, key_scale, map_scale),
        grid=(1,),
        in_specs=[full] * 4
        + [pl.BlockSpec((heads, length), lambda i: (0, 0))]
        + [pl.BlockSpec((heads, width, width), lambda i: (0, 0, 0))] * 2,
        out_specs=[full] * 4 + [anywhere] * 2,
        out_shape=[wide_shape] * 2 + [sum_shape] * 2 + [half_shape] * 2,
        scratch_shapes=[pltpu.VMEM((2, 2, near, quarter, width), BF16), pltpu.SemaphoreType.DMA((4,))],
        cost_estimate=pl.CostEstimate(flops=7 * flops, bytes_accessed=8 << 20, transcendentals=1 << 18),
    )(q, k, v, g, gates, query_map, key_map)
    received, keep = lax.optimization_barrier((received, keep))
    swap = [(0, 1), (1, 0)]
    whole = pl.BlockSpec(memory_space=pltpu.VMEM)
    part = jax.ShapeDtypeStruct((near, quarter, width), BF16)
    keep, send = pl.pallas_call(
        halve_kernel, in_specs=[whole] * 2, out_shape=[part] * 2, compiler_params=VMEM
    )(keep, lax.ppermute(send, "core", swap))
    totals = pl.pallas_call(
        functools.partial(totals_kernel, key_scale),
        in_specs=[whole] * 3,
        out_shape=jax.ShapeDtypeStruct((outer, share, width + 2 * PAD, width), BF16),
        compiler_params=VMEM,
    )(received, query_map, key_map)
    blocks = pl.pallas_call(
        functools.partial(blocks_kernel, key_scale),
        in_specs=[whole] * 3,
        out_shape=jax.ShapeDtypeStruct((near, share, 2 * width, width), BF16),
        cost_estimate=pl.CostEstimate(flops=2 * flops, bytes_accessed=2 << 20, transcendentals=0),
        compiler_params=VMEM,
    )(received, query_map, key_map)
    totals, send = lax.optimization_barrier((exchange(totals, "outer"), send))
    inside_got = lax.ppermute(send, "y_lo", swap)
    states, owned = pl.pallas_call(
        functools.partial(spread_kernel, key_scale, map_scale),
        in_specs=[whole] * 3,
        out_shape=[
            jax.ShapeDtypeStruct((near, rows, width), BF16),
            jax.ShapeDtypeStruct((2, near, 32, width), BF16),
        ],
        compiler_params=VMEM,
    )(received, blocks, totals)
    carried = exchange(states, NEAR)
    maps = pl.pallas_call(
        pair_kernel,
        in_specs=[whole] * 4,
        out_shape=jax.ShapeDtypeStruct((near, quarter + 32, width), BF16),
        compiler_params=VMEM,
    )(keep, inside_got, owned, lax.ppermute(owned[1], "core", swap))
    carried, maps = lax.optimization_barrier((carried, maps))
    maps = pl.pallas_call(
        gather_kernel,
        in_specs=[whole],
        out_shape=jax.ShapeDtypeStruct((2, 2, 2, 32, width), BF16),
        compiler_params=VMEM,
    )(exchange(maps, NEAR))
    maps = exchange(maps.reshape(32, 8, width), ("y_hi", "y_lo", "outer"))
    query_grad, key_grad, value_grad = pl.pallas_call(
        functools.partial(grads_kernel, key_scale),
        grid=(steps,),
        in_specs=[wide] * 4 + [gate_spec, map_spec, map_spec] + [wide] * 2
        + [pl.BlockSpec((near // steps, rows, width), lambda i: (i, 0, 0))],
        out_specs=[wide] * 3,
        out_shape=[wide_shape] * 3,
        cost_estimate=pl.CostEstimate(flops=7 * flops, bytes_accessed=8 << 20, transcendentals=0),
    )(v, g, fq, fk, gates, query_map, key_map, query_inside, key_inside, carried)
    map_grads = add_up(maps, F32)
    shape = queries.shape
    return query_grad.reshape(shape), key_grad.reshape(shape), value_grad.reshape(shape), map_grads


def solution(mesh):
    fine = Mesh(np.asarray(mesh.devices).reshape(4, 2, 2, 4, 2, 4), DP + CONTEXT)
    split = P(DP, CONTEXT, None)
    return jax.shard_map(
        per_device,
        mesh=fine,
        in_specs=(split, split, split, split, P(DP, None, CONTEXT), P(), P()),
        out_specs=(split, split, split, P(DP + CONTEXT, None)),
        check_vma=False,
    )
```

```python
import functools

import jax
import jax.numpy as jnp
import numpy as np
from jax import lax
from jax.experimental import pallas as pl
from jax.experimental.pallas import tpu as pltpu
from jax.sharding import Mesh, PartitionSpec as P

F32 = jnp.float32
BF16 = jnp.bfloat16
GROUP = 8
PAD = 8
DP = ("y_hi", "y_lo", "core")
CONTEXT = ("outer", "inner", "x")
NEAR = ("inner", "x")
VMEM = pltpu.CompilerParams(vmem_limit_bytes=20 << 20)


def dot(a, b, contract, precision=None):
    return lax.dot_general(
        a, b, ((contract[:1], contract[1:]), ((), ())), precision=precision, preferred_element_type=F32
    )


def place(head):
    return 2 * (head // 4) + head % 2, (head // 2) % 2


def causal_mask(length):
    t = lax.broadcasted_iota(jnp.int32, (length, length), 0)
    s = lax.broadcasted_iota(jnp.int32, (length, length), 1)
    return t >= s


def running_columns(gates):
    lower = jnp.where(causal_mask(gates.shape[1]), 1.0, 0.0).astype(F32)
    return dot(lower, gates, (1, 1), lax.Precision.HIGHEST)


def running_rows(gates):
    lower = jnp.where(causal_mask(gates.shape[1]), 1.0, 0.0).astype(F32)
    return dot(gates, lower, (1, 1), lax.Precision.HIGHEST)


def products_kernel(q_ref, k_ref, v_ref, g_ref, gates_ref, out_ref):
    length = q_ref.shape[0]
    width = q_ref.shape[1] // GROUP
    columns = running_columns(gates_ref[...])
    for j in range(GROUP):
        lanes = slice(j * width, (j + 1) * width)
        owner, bit = place(j)
        run = columns[:, j : j + 1]
        closing = run[length - 1 : length]
        g_start = (g_ref[:, lanes].astype(F32) * jnp.exp(run)).astype(BF16)
        v_end = (v_ref[:, lanes].astype(F32) * jnp.exp(closing - run)).astype(BF16)
        to = 2 * owner + bit
        out_ref[to, 0:width] = dot(q_ref[:, lanes], g_start, (0, 0)).astype(BF16)
        out_ref[to, width : 2 * width] = dot(k_ref[:, lanes], v_end, (0, 0)).astype(BF16)
        out_ref[to, 2 * width :] = jnp.broadcast_to(closing, (PAD, width)).astype(BF16)


def owned_heads():
    x = lax.axis_index("x")
    return (lax.axis_index("inner") * 2 + x // 2) * 4 + x % 2


def inside_kernel(
    key_scale, map_scale, q_ref, k_ref, v_ref, g_ref, gates_ref, mq_ref, mk_ref,
    fq_ref, fk_ref, qb_ref, kb_ref, keep_ref, send_ref, maps_ref, sems,
):
    heads, width = mq_ref.shape[0], mq_ref.shape[1]
    causal = causal_mask(q_ref.shape[0])
    columns = running_columns(gates_ref[...])
    rows = running_rows(gates_ref[...])
    for j in range(heads):
        lanes = slice(j * width, (j + 1) * width)
        owner, bit = place(j)
        within = jnp.exp(jnp.where(causal, columns[:, j : j + 1] - rows[j : j + 1], -1e30))
        q, k, v, g = q_ref[:, lanes], k_ref[:, lanes], v_ref[:, lanes], g_ref[:, lanes]
        fq = dot(q, mq_ref[j], (1, 0)).astype(BF16)
        fk = (dot(k, mk_ref[j], (1, 0)) * key_scale).astype(BF16)
        grad_scores = (dot(g, v, (1, 1)) * within).astype(BF16)
        query_back = dot(grad_scores, fk, (1, 0))
        key_back = dot(grad_scores, fq, (0, 0)) * key_scale
        fq_ref[:, lanes] = fq
        fk_ref[:, lanes] = fk
        qb_ref[:, lanes] = query_back
        kb_ref[:, lanes] = key_back
        for m, (x, back) in enumerate(((q, query_back), (k, key_back))):
            part = dot(x, back.astype(BF16), (0, 0)) * map_scale
            at = ((m * 2 + owner // 4) * 2 + owner % 2) * 16
            for b in range(width // 8):
                to = at + (b // 8) * 8
                maps_ref[bit, (owner // 2) % 2, b % 8, to : to + 8] = part[8 * b : 8 * b + 8].astype(BF16)
    core, y_lo = lax.axis_index("core"), lax.axis_index("y_lo")
    copies = []
    for side in range(2):
        along = lax.bitwise_xor(y_lo, side)
        copies.append(pltpu.make_async_copy(maps_ref.at[core, along], keep_ref.at[side], sems.at[2 * side]))
        copies.append(pltpu.make_async_copy(maps_ref.at[1 - core, along], send_ref.at[side], sems.at[2 * side + 1]))
    for copy in copies:
        copy.start()
    for copy in copies:
        copy.wait()


def over(decay, value):
    rows, width = value.shape
    return (decay[None] * value.reshape(rows // PAD, PAD, width)).reshape(rows, width)


def decay_of(ref, r, h, width):
    return jnp.exp(ref[r, h, 2 * width :].astype(F32))


def block_state(key_scale, in_ref, map_ref, head, r, h, width):
    return dot(map_ref[head], in_ref[r, h, width : 2 * width], (0, 0)) * key_scale


def block_grad(in_ref, map_ref, head, r, h, width):
    return dot(map_ref[head], in_ref[r, h, 0:width], (0, 0))


def totals_kernel(key_scale, in_ref, mq_ref, mk_ref, out_ref):
    near, heads, width = in_ref.shape[0], in_ref.shape[1], in_ref.shape[3]
    mine = lax.axis_index("outer")
    for h in range(heads):
        head = owned_heads() + 2 * h
        ahead = jnp.zeros((width, width), F32)
        back = jnp.zeros((width, width), F32)
        log = jnp.zeros((PAD, width), F32)
        for r in range(near):
            b = near - 1 - r
            state = block_state(key_scale, in_ref, mk_ref, head, r, h, width)
            ahead = over(decay_of(in_ref, r, h, width), ahead) + state
            back = over(decay_of(in_ref, b, h, width), back) + block_grad(in_ref, mq_ref, head, b, h, width)
            log = log + in_ref[r, h, 2 * width :].astype(F32)
        coarse = log.astype(BF16)
        fine = (log - coarse.astype(F32)).astype(BF16)
        for o in range(out_ref.shape[0]):
            out_ref[o, h, 0:width] = jnp.where(o > mine, ahead, back).astype(BF16)
            out_ref[o, h, width : width + PAD] = coarse
            out_ref[o, h, width + PAD :] = fine


def blocks_kernel(key_scale, in_ref, mq_ref, mk_ref, out_ref):
    near, heads, width = in_ref.shape[0], in_ref.shape[1], in_ref.shape[3]
    for h in range(heads):
        head = owned_heads() + 2 * h
        for r in range(near):
            out_ref[r, h, 0:width] = block_state(key_scale, in_ref, mk_ref, head, r, h, width).astype(BF16)
            out_ref[r, h, width:] = block_grad(in_ref, mq_ref, head, r, h, width).astype(BF16)


def spread_kernel(key_scale, map_scale, in_ref, blocks_ref, totals_ref, states_ref, maps_ref):
    near, heads, width = in_ref.shape[0], in_ref.shape[1], in_ref.shape[3]
    groups = totals_ref.shape[0]
    mine, core = lax.axis_index("outer"), lax.axis_index("core")

    def total(o, h):
        log = totals_ref[o, h, width : width + PAD].astype(F32) + totals_ref[o, h, width + PAD :].astype(F32)
        return jnp.exp(log), totals_ref[o, h, 0:width].astype(F32)

    for h in range(heads):
        ahead = jnp.zeros((width, width), F32)
        back = jnp.zeros((width, width), F32)
        for o in range(groups):
            decay, value = total(o, h)
            ahead = jnp.where(o < mine, over(decay, ahead) + value, ahead)
            b = groups - 1 - o
            decay, value = total(b, h)
            back = jnp.where(b > mine, over(decay, back) + value, back)
        sums = [jnp.zeros((width, width), F32), jnp.zeros((width, width), F32)]
        for r in range(near):
            b = near - 1 - r
            state_in, grad_in = ahead.astype(BF16), back.astype(BF16)
            states_ref[r, 2 * h * width : (2 * h + 1) * width] = state_in
            states_ref[b, (2 * h + 1) * width : (2 * h + 2) * width] = grad_in
            sums[0] = sums[0] + dot(in_ref[r, h, 0:width], state_in, (1, 1))
            sums[1] = sums[1] + dot(in_ref[b, h, width : 2 * width], grad_in, (1, 1))
            if r < near - 1:
                ahead = over(decay_of(in_ref, r, h, width), ahead) + blocks_ref[r, h, 0:width].astype(F32)
                back = over(decay_of(in_ref, b, h, width), back) + blocks_ref[b, h, width:].astype(F32)
        side = lax.bitwise_xor(core, h)
        for m, scale in enumerate((map_scale, map_scale * key_scale)):
            part = sums[m] * scale
            for b in range(width // 8):
                to = (m * 2 + b // 8) * 8
                maps_ref[side, b % 8, to : to + 8] = part[8 * b : 8 * b + 8].astype(BF16)


def halve_kernel(kept_ref, got_ref, keep_ref, send_ref):
    keep_ref[...] = (kept_ref[0].astype(F32) + got_ref[0].astype(F32)).astype(BF16)
    send_ref[...] = (kept_ref[1].astype(F32) + got_ref[1].astype(F32)).astype(BF16)


def pair_kernel(inside_ref, inside_got_ref, carried_ref, carried_got_ref, out_ref):
    rows = inside_ref.shape[1]
    out_ref[:, 0:rows] = (inside_ref[...].astype(F32) + inside_got_ref[...].astype(F32)).astype(BF16)
    out_ref[:, rows:] = (carried_ref[0].astype(F32) + carried_got_ref[...].astype(F32)).astype(BF16)


def gather_kernel(in_ref, out_ref):
    y_lo = lax.axis_index("y_lo")
    rows = in_ref.shape[1] - 32
    for r in range(in_ref.shape[0]):
        for m in range(2):
            of, to = rows + m * 16, (r % 2) * 16
            out_ref[m, r // 4, (r // 2) % 2, to : to + 16] = in_ref[r, of : of + 16]
    total = jnp.sum(in_ref[:, 0:rows].astype(F32), axis=0)
    for m in range(2):
        for high in range(2):
            at = (m * 2 + high) * 32
            here = out_ref[m, high, y_lo].astype(F32)
            out_ref[m, high, y_lo] = (here + total[at : at + 32]).astype(BF16)


def grads_kernel(
    key_scale, v_ref, g_ref, fq_ref, fk_ref, gates_ref, mq_ref, mk_ref, qb_ref, kb_ref, in_ref, qg_ref, kg_ref, vg_ref
):
    width = mq_ref.shape[1]
    length = fk_ref.shape[0]
    causal = causal_mask(length)
    columns = running_columns(gates_ref[...])
    rows = running_rows(gates_ref[...])
    for j in range(GROUP):
        lanes = slice(j * width, (j + 1) * width)
        owner, bit = place(j)
        run = columns[:, j : j + 1]
        within = jnp.exp(jnp.where(causal, run - rows[j : j + 1], -1e30))
        start = jnp.exp(run)
        end = jnp.exp(run[length - 1 : length] - run)
        state_in = in_ref[owner, 2 * bit * width : (2 * bit + 1) * width]
        grad_in = in_ref[owner, (2 * bit + 1) * width : (2 * bit + 2) * width]
        g, fk = g_ref[:, lanes], fk_ref[:, lanes]
        scores = (dot(fq_ref[:, lanes], fk, (1, 1)) * within).astype(BF16)
        query_back = (qb_ref[:, lanes] + dot(g, state_in, (1, 1)) * start).astype(BF16)
        key_back = (kb_ref[:, lanes] + dot(v_ref[:, lanes], grad_in, (1, 1)) * (end * key_scale)).astype(BF16)
        vg_ref[:, lanes] = (dot(scores, g, (0, 0)) + dot(fk, grad_in, (1, 0)) * end).astype(BF16)
        qg_ref[:, lanes] = dot(query_back, mq_ref[j], (1, 1)).astype(BF16)
        kg_ref[:, lanes] = dot(key_back, mk_ref[j], (1, 1)).astype(BF16)


def sum_kernel(in_ref, out_ref):
    out_ref[...] = jnp.sum(in_ref[...].astype(F32), axis=0).astype(out_ref.dtype)


def add_up(value, dtype):
    out_shape = jax.ShapeDtypeStruct(value.shape[1:], dtype)
    return pl.pallas_call(sum_kernel, out_shape=out_shape, compiler_params=VMEM)(value)


def exchange(value, axes):
    return lax.all_to_all(value, axes, 0, 0, tiled=True)


def per_device(queries, keys, values, out_grad, log_gates, query_map, key_map):
    heads, width = query_map.shape[0], query_map.shape[1]
    length = queries.shape[1]
    near, outer = lax.axis_size(NEAR), lax.axis_size("outer")
    key_scale = width ** (-0.5) / 16.0
    map_scale = (lax.axis_size(DP) * lax.axis_size(CONTEXT) * length) ** (-0.5)
    steps = heads // GROUP
    share = heads // near
    q, k, v, g = (x.reshape(length, heads * width) for x in (queries, keys, values, out_grad))
    gates = log_gates.reshape(heads, length)
    wide = pl.BlockSpec((length, GROUP * width), lambda i: (0, i))
    gate_spec = pl.BlockSpec((GROUP, length), lambda i: (i, 0))
    map_spec = pl.BlockSpec((GROUP, width, width), lambda i: (i, 0, 0))
    wide_shape = jax.ShapeDtypeStruct((length, heads * width), BF16)
    sum_shape = jax.ShapeDtypeStruct((length, heads * width), F32)
    flops = 2 * length * width * width * heads
    sent = pl.pallas_call(
        products_kernel,
        grid=(steps,),
        in_specs=[wide, wide, wide, wide, gate_spec],
        out_specs=pl.BlockSpec((GROUP, 2 * width + PAD, width), lambda i: (i, 0, 0)),
        out_shape=jax.ShapeDtypeStruct((heads, 2 * width + PAD, width), BF16),
        cost_estimate=pl.CostEstimate(flops=2 * flops, bytes_accessed=3 << 20, transcendentals=0),
    )(q, k, v, g, gates)
    received = exchange(sent.reshape(near, share, 2 * width + PAD, width), NEAR)
    rows, quarter = 2 * share * width, heads * 8
    full = pl.BlockSpec((length, heads * width), lambda i: (0, 0))
    half_shape = jax.ShapeDtypeStruct((2, near, quarter, width), BF16)
    anywhere = pl.BlockSpec(memory_space=pl.ANY)
    fq, fk, query_inside, key_inside, keep, send = pl.pallas_call(
        functools.partial(inside_kernel, key_scale, map_scale),
        grid=(1,),
        in_specs=[full] * 4
        + [pl.BlockSpec((heads, length), lambda i: (0, 0))]
        + [pl.BlockSpec((heads, width, width), lambda i: (0, 0, 0))] * 2,
        out_specs=[full] * 4 + [anywhere] * 2,
        out_shape=[wide_shape] * 2 + [sum_shape] * 2 + [half_shape] * 2,
        scratch_shapes=[pltpu.VMEM((2, 2, near, quarter, width), BF16), pltpu.SemaphoreType.DMA((4,))],
        cost_estimate=pl.CostEstimate(flops=7 * flops, bytes_accessed=8 << 20, transcendentals=1 << 18),
    )(q, k, v, g, gates, query_map, key_map)
    received, keep = lax.optimization_barrier((received, keep))
    swap = [(0, 1), (1, 0)]
    whole = pl.BlockSpec(memory_space=pltpu.VMEM)
    part = jax.ShapeDtypeStruct((near, quarter, width), BF16)
    keep, send = pl.pallas_call(
        halve_kernel, in_specs=[whole] * 2, out_shape=[part] * 2, compiler_params=VMEM
    )(keep, lax.ppermute(send, "core", swap))
    totals = pl.pallas_call(
        functools.partial(totals_kernel, key_scale),
        in_specs=[whole] * 3,
        out_shape=jax.ShapeDtypeStruct((outer, share, width + 2 * PAD, width), BF16),
        compiler_params=VMEM,
    )(received, query_map, key_map)
    blocks = pl.pallas_call(
        functools.partial(blocks_kernel, key_scale),
        in_specs=[whole] * 3,
        out_shape=jax.ShapeDtypeStruct((near, share, 2 * width, width), BF16),
        cost_estimate=pl.CostEstimate(flops=2 * flops, bytes_accessed=2 << 20, transcendentals=0),
        compiler_params=VMEM,
    )(received, query_map, key_map)
    inside_got = lax.ppermute(send, "y_lo", swap)
    totals, inside_got = lax.optimization_barrier((exchange(totals, "outer"), inside_got))
    states, owned = pl.pallas_call(
        functools.partial(spread_kernel, key_scale, map_scale),
        in_specs=[whole] * 3,
        out_shape=[
            jax.ShapeDtypeStruct((near, rows, width), BF16),
            jax.ShapeDtypeStruct((2, near, 32, width), BF16),
        ],
        compiler_params=VMEM,
    )(received, blocks, totals)
    carried = exchange(states, NEAR)
    maps = pl.pallas_call(
        pair_kernel,
        in_specs=[whole] * 4,
        out_shape=jax.ShapeDtypeStruct((near, quarter + 32, width), BF16),
        compiler_params=VMEM,
    )(keep, inside_got, owned, lax.ppermute(owned[1], "core", swap))
    carried, maps = lax.optimization_barrier((carried, maps))
    query_grad, key_grad, value_grad = pl.pallas_call(
        functools.partial(grads_kernel, key_scale),
        grid=(steps,),
        in_specs=[wide] * 4 + [gate_spec, map_spec, map_spec] + [wide] * 2
        + [pl.BlockSpec((near // steps, rows, width), lambda i: (i, 0, 0))],
        out_specs=[wide] * 3,
        out_shape=[wide_shape] * 3,
        cost_estimate=pl.CostEstimate(flops=7 * flops, bytes_accessed=8 << 20, transcendentals=0),
    )(v, g, fq, fk, gates, query_map, key_map, query_inside, key_inside, carried)
    maps, query_grad = lax.optimization_barrier((exchange(maps, NEAR), query_grad))
    maps = pl.pallas_call(
        gather_kernel,
        in_specs=[whole],
        out_shape=jax.ShapeDtypeStruct((2, 2, 2, 32, width), BF16),
        compiler_params=VMEM,
    )(maps)
    maps = exchange(maps.reshape(32, 8, width), ("y_hi", "y_lo", "outer"))
    map_grads = add_up(maps, F32)
    shape = queries.shape
    return query_grad.reshape(shape), key_grad.reshape(shape), value_grad.reshape(shape), map_grads


def solution(mesh):
    fine = Mesh(np.asarray(mesh.devices).reshape(4, 2, 2, 4, 2, 4), DP + CONTEXT)
    split = P(DP, CONTEXT, None)
    return jax.shard_map(
        per_device,
        mesh=fine,
        in_specs=(split, split, split, split, P(DP, None, CONTEXT), P(), P()),
        out_specs=(split, split, split, P(DP + CONTEXT, None)),
        check_vma=False,
    )
```

```python
import functools

import jax
import jax.numpy as jnp
import numpy as np
from jax import lax
from jax.experimental import pallas as pl
from jax.experimental.pallas import tpu as pltpu
from jax.sharding import Mesh, PartitionSpec as P

F32 = jnp.float32
BF16 = jnp.bfloat16
GROUP = 8
PAD = 8
DP = ("y_hi", "y_lo", "core")
CONTEXT = ("outer", "inner", "x")
NEAR = ("inner", "x")
VMEM = pltpu.CompilerParams(vmem_limit_bytes=20 << 20)


def dot(a, b, contract, precision=None):
    return lax.dot_general(
        a, b, ((contract[:1], contract[1:]), ((), ())), precision=precision, preferred_element_type=F32
    )


def place(head):
    return 2 * (head // 4) + head % 2, (head // 2) % 2


def causal_mask(length):
    t = lax.broadcasted_iota(jnp.int32, (length, length), 0)
    s = lax.broadcasted_iota(jnp.int32, (length, length), 1)
    return t >= s


def running_columns(gates):
    lower = jnp.where(causal_mask(gates.shape[1]), 1.0, 0.0).astype(F32)
    return dot(lower, gates, (1, 1), lax.Precision.HIGHEST)


def running_rows(gates):
    lower = jnp.where(causal_mask(gates.shape[1]), 1.0, 0.0).astype(F32)
    return dot(gates, lower, (1, 1), lax.Precision.HIGHEST)


def products_kernel(q_ref, k_ref, v_ref, g_ref, gates_ref, out_ref):
    length = q_ref.shape[0]
    width = q_ref.shape[1] // GROUP
    columns = running_columns(gates_ref[...])
    for j in range(GROUP):
        lanes = slice(j * width, (j + 1) * width)
        owner, bit = place(j)
        run = columns[:, j : j + 1]
        closing = run[length - 1 : length]
        g_start = (g_ref[:, lanes].astype(F32) * jnp.exp(run)).astype(BF16)
        v_end = (v_ref[:, lanes].astype(F32) * jnp.exp(closing - run)).astype(BF16)
        to = 2 * owner + bit
        out_ref[to, 0:width] = dot(q_ref[:, lanes], g_start, (0, 0)).astype(BF16)
        out_ref[to, width : 2 * width] = dot(k_ref[:, lanes], v_end, (0, 0)).astype(BF16)
        out_ref[to, 2 * width :] = jnp.broadcast_to(closing, (PAD, width)).astype(BF16)


def owned_heads():
    x = lax.axis_index("x")
    return (lax.axis_index("inner") * 2 + x // 2) * 4 + x % 2


def inside_kernel(
    key_scale, map_scale, q_ref, k_ref, v_ref, g_ref, gates_ref, mq_ref, mk_ref,
    fq_ref, fk_ref, qb_ref, kb_ref, keep_ref, send_ref, maps_ref, sems,
):
    heads, width = mq_ref.shape[0], mq_ref.shape[1]
    step = pl.program_id(0)
    causal = causal_mask(q_ref.shape[0])
    columns = running_columns(gates_ref[...])
    rows = running_rows(gates_ref[...])
    for j in range(heads):
        lanes = slice(j * width, (j + 1) * width)
        owner, bit = place(j)
        within = jnp.exp(jnp.where(causal, columns[:, j : j + 1] - rows[j : j + 1], -1e30))
        q, k, v, g = q_ref[:, lanes], k_ref[:, lanes], v_ref[:, lanes], g_ref[:, lanes]
        fq = dot(q, mq_ref[j], (1, 0)).astype(BF16)
        fk = (dot(k, mk_ref[j], (1, 0)) * key_scale).astype(BF16)
        grad_scores = (dot(g, v, (1, 1)) * within).astype(BF16)
        query_back = dot(grad_scores, fk, (1, 0))
        key_back = dot(grad_scores, fq, (0, 0)) * key_scale
        fq_ref[:, lanes] = fq
        fk_ref[:, lanes] = fk
        qb_ref[:, lanes] = query_back
        kb_ref[:, lanes] = key_back
        for m, (x, back) in enumerate(((q, query_back), (k, key_back))):
            part = dot(x, back.astype(BF16), (0, 0)) * map_scale
            for b in range(width // 8):
                to = (owner % 2) * 16 + (b // 8) * 8
                maps_ref[bit, (owner // 2) % 2, b % 8, m, step, to : to + 8] = part[8 * b : 8 * b + 8].astype(BF16)

    @pl.when(step == pl.num_programs(0) - 1)
    def _():
        core, y_lo = lax.axis_index("core"), lax.axis_index("y_lo")
        copies = []
        for side in range(2):
            along = lax.bitwise_xor(y_lo, side)
            for to, (ref, of) in enumerate(((keep_ref, core), (send_ref, 1 - core))):
                copies.append(pltpu.make_async_copy(maps_ref.at[of, along], ref.at[side], sems.at[2 * side + to]))
        for copy in copies:
            copy.start()
        for copy in copies:
            copy.wait()


def over(decay, value):
    rows, width = value.shape
    return (decay[None] * value.reshape(rows // PAD, PAD, width)).reshape(rows, width)


def decay_of(ref, r, h, width):
    return jnp.exp(ref[r, h, 2 * width :].astype(F32))


def block_state(key_scale, in_ref, map_ref, head, r, h, width):
    return dot(map_ref[head], in_ref[r, h, width : 2 * width], (0, 0)) * key_scale


def block_grad(in_ref, map_ref, head, r, h, width):
    return dot(map_ref[head], in_ref[r, h, 0:width], (0, 0))


def totals_kernel(key_scale, in_ref, mq_ref, mk_ref, out_ref):
    near, heads, width = in_ref.shape[0], in_ref.shape[1], in_ref.shape[3]
    mine = lax.axis_index("outer")
    for h in range(heads):
        head = owned_heads() + 2 * h
        ahead = jnp.zeros((width, width), F32)
        back = jnp.zeros((width, width), F32)
        log = jnp.zeros((PAD, width), F32)
        for r in range(near):
            b = near - 1 - r
            state = block_state(key_scale, in_ref, mk_ref, head, r, h, width)
            ahead = over(decay_of(in_ref, r, h, width), ahead) + state
            back = over(decay_of(in_ref, b, h, width), back) + block_grad(in_ref, mq_ref, head, b, h, width)
            log = log + in_ref[r, h, 2 * width :].astype(F32)
        coarse = log.astype(BF16)
        fine = (log - coarse.astype(F32)).astype(BF16)
        for o in range(out_ref.shape[0]):
            out_ref[o, h, 0:width] = jnp.where(o > mine, ahead, back).astype(BF16)
            out_ref[o, h, width : width + PAD] = coarse
            out_ref[o, h, width + PAD :] = fine


def blocks_kernel(key_scale, in_ref, mq_ref, mk_ref, out_ref):
    near, heads, width = in_ref.shape[0], in_ref.shape[1], in_ref.shape[3]
    for h in range(heads):
        head = owned_heads() + 2 * h
        for r in range(near):
            out_ref[r, h, 0:width] = block_state(key_scale, in_ref, mk_ref, head, r, h, width).astype(BF16)
            out_ref[r, h, width:] = block_grad(in_ref, mq_ref, head, r, h, width).astype(BF16)


def spread_kernel(key_scale, map_scale, in_ref, blocks_ref, totals_ref, states_ref, maps_ref):
    near, heads, width = in_ref.shape[0], in_ref.shape[1], in_ref.shape[3]
    groups = totals_ref.shape[0]
    mine, core = lax.axis_index("outer"), lax.axis_index("core")

    def total(o, h):
        log = totals_ref[o, h, width : width + PAD].astype(F32) + totals_ref[o, h, width + PAD :].astype(F32)
        return jnp.exp(log), totals_ref[o, h, 0:width].astype(F32)

    for h in range(heads):
        ahead = jnp.zeros((width, width), F32)
        back = jnp.zeros((width, width), F32)
        for o in range(groups):
            decay, value = total(o, h)
            ahead = jnp.where(o < mine, over(decay, ahead) + value, ahead)
            b = groups - 1 - o
            decay, value = total(b, h)
            back = jnp.where(b > mine, over(decay, back) + value, back)
        sums = [jnp.zeros((width, width), F32), jnp.zeros((width, width), F32)]
        for r in range(near):
            b = near - 1 - r
            state_in, grad_in = ahead.astype(BF16), back.astype(BF16)
            states_ref[r, 2 * h * width : (2 * h + 1) * width] = state_in
            states_ref[b, (2 * h + 1) * width : (2 * h + 2) * width] = grad_in
            sums[0] = sums[0] + dot(in_ref[r, h, 0:width], state_in, (1, 1))
            sums[1] = sums[1] + dot(in_ref[b, h, width : 2 * width], grad_in, (1, 1))
            if r < near - 1:
                ahead = over(decay_of(in_ref, r, h, width), ahead) + blocks_ref[r, h, 0:width].astype(F32)
                back = over(decay_of(in_ref, b, h, width), back) + blocks_ref[b, h, width:].astype(F32)
        side = lax.bitwise_xor(core, h)
        for m, scale in enumerate((map_scale, map_scale * key_scale)):
            part = sums[m] * scale
            for b in range(width // 8):
                to = (m * 2 + b // 8) * 8
                maps_ref[side, b % 8, to : to + 8] = part[8 * b : 8 * b + 8].astype(BF16)


def halve_kernel(kept_ref, got_ref, keep_ref, send_ref):
    keep_ref[...] = (kept_ref[0].astype(F32) + got_ref[0].astype(F32)).astype(BF16)
    send_ref[...] = (kept_ref[1].astype(F32) + got_ref[1].astype(F32)).astype(BF16)


def pair_kernel(inside_ref, inside_got_ref, carried_ref, carried_got_ref, out_ref):
    rows = inside_ref.shape[1]
    out_ref[:, 0:rows] = (inside_ref[...].astype(F32) + inside_got_ref[...].astype(F32)).astype(BF16)
    out_ref[:, rows:] = (carried_ref[0].astype(F32) + carried_got_ref[...].astype(F32)).astype(BF16)


def gather_kernel(in_ref, out_ref):
    y_lo = lax.axis_index("y_lo")
    rows = in_ref.shape[1] - 32
    for r in range(in_ref.shape[0]):
        for m in range(2):
            of, to = rows + m * 16, (r % 2) * 16
            out_ref[m, r // 4, (r // 2) % 2, to : to + 16] = in_ref[r, of : of + 16]
    total = jnp.sum(in_ref[:, 0:rows].astype(F32), axis=0)
    for m in range(2):
        for high in range(2):
            at = (m * 2 + high) * 32
            here = out_ref[m, high, y_lo].astype(F32)
            out_ref[m, high, y_lo] = (here + total[at : at + 32]).astype(BF16)


def grads_kernel(
    key_scale, v_ref, g_ref, fq_ref, fk_ref, gates_ref, mq_ref, mk_ref, qb_ref, kb_ref, in_ref, qg_ref, kg_ref, vg_ref
):
    width = mq_ref.shape[1]
    length = fk_ref.shape[0]
    causal = causal_mask(length)
    columns = running_columns(gates_ref[...])
    rows = running_rows(gates_ref[...])
    for j in range(GROUP):
        lanes = slice(j * width, (j + 1) * width)
        owner, bit = place(j)
        run = columns[:, j : j + 1]
        within = jnp.exp(jnp.where(causal, run - rows[j : j + 1], -1e30))
        start = jnp.exp(run)
        end = jnp.exp(run[length - 1 : length] - run)
        state_in = in_ref[owner, 2 * bit * width : (2 * bit + 1) * width]
        grad_in = in_ref[owner, (2 * bit + 1) * width : (2 * bit + 2) * width]
        g, fk = g_ref[:, lanes], fk_ref[:, lanes]
        scores = (dot(fq_ref[:, lanes], fk, (1, 1)) * within).astype(BF16)
        query_back = (qb_ref[:, lanes] + dot(g, state_in, (1, 1)) * start).astype(BF16)
        key_back = (kb_ref[:, lanes] + dot(v_ref[:, lanes], grad_in, (1, 1)) * (end * key_scale)).astype(BF16)
        vg_ref[:, lanes] = (dot(scores, g, (0, 0)) + dot(fk, grad_in, (1, 0)) * end).astype(BF16)
        qg_ref[:, lanes] = dot(query_back, mq_ref[j], (1, 1)).astype(BF16)
        kg_ref[:, lanes] = dot(key_back, mk_ref[j], (1, 1)).astype(BF16)


def sum_kernel(in_ref, out_ref):
    out_ref[...] = jnp.sum(in_ref[...].astype(F32), axis=0).astype(out_ref.dtype)


def add_up(value, dtype):
    out_shape = jax.ShapeDtypeStruct(value.shape[1:], dtype)
    return pl.pallas_call(sum_kernel, out_shape=out_shape, compiler_params=VMEM)(value)


def exchange(value, axes):
    return lax.all_to_all(value, axes, 0, 0, tiled=True)


def per_device(queries, keys, values, out_grad, log_gates, query_map, key_map):
    heads, width = query_map.shape[0], query_map.shape[1]
    length = queries.shape[1]
    near, outer = lax.axis_size(NEAR), lax.axis_size("outer")
    key_scale = width ** (-0.5) / 16.0
    map_scale = (lax.axis_size(DP) * lax.axis_size(CONTEXT) * length) ** (-0.5)
    steps = heads // GROUP
    share = heads // near
    q, k, v, g = (x.reshape(length, heads * width) for x in (queries, keys, values, out_grad))
    gates = log_gates.reshape(heads, length)
    wide = pl.BlockSpec((length, GROUP * width), lambda i: (0, i))
    gate_spec = pl.BlockSpec((GROUP, length), lambda i: (i, 0))
    map_spec = pl.BlockSpec((GROUP, width, width), lambda i: (i, 0, 0))
    wide_shape = jax.ShapeDtypeStruct((length, heads * width), BF16)
    sum_shape = jax.ShapeDtypeStruct((length, heads * width), F32)
    flops = 2 * length * width * width * heads
    sent = pl.pallas_call(
        products_kernel,
        grid=(steps,),
        in_specs=[wide, wide, wide, wide, gate_spec],
        out_specs=pl.BlockSpec((GROUP, 2 * width + PAD, width), lambda i: (i, 0, 0)),
        out_shape=jax.ShapeDtypeStruct((heads, 2 * width + PAD, width), BF16),
        cost_estimate=pl.CostEstimate(flops=2 * flops, bytes_accessed=3 << 20, transcendentals=0),
    )(q, k, v, g, gates)
    received = exchange(sent.reshape(near, share, 2 * width + PAD, width), NEAR)
    rows, quarter = 2 * share * width, heads * 8
    half_shape = jax.ShapeDtypeStruct((2, near, 2, steps, 32, width), BF16)
    anywhere = pl.BlockSpec(memory_space=pl.ANY)
    fq, fk, query_inside, key_inside, keep, send = pl.pallas_call(
        functools.partial(inside_kernel, key_scale, map_scale),
        grid=(steps,),
        in_specs=[wide] * 4 + [gate_spec, map_spec, map_spec],
        out_specs=[wide] * 4 + [anywhere] * 2,
        out_shape=[wide_shape] * 2 + [sum_shape] * 2 + [half_shape] * 2,
        scratch_shapes=[pltpu.VMEM((2, 2, near, 2, steps, 32, width), BF16), pltpu.SemaphoreType.DMA((4,))],
        cost_estimate=pl.CostEstimate(flops=7 * flops, bytes_accessed=8 << 20, transcendentals=1 << 18),
    )(q, k, v, g, gates, query_map, key_map)
    keep, send = (x.reshape(2, near, quarter, width) for x in (keep, send))
    received, keep = lax.optimization_barrier((received, keep))
    swap = [(0, 1), (1, 0)]
    whole = pl.BlockSpec(memory_space=pltpu.VMEM)
    part = jax.ShapeDtypeStruct((near, quarter, width), BF16)
    totals = pl.pallas_call(
        functools.partial(totals_kernel, key_scale),
        in_specs=[whole] * 3,
        out_shape=jax.ShapeDtypeStruct((outer, share, width + 2 * PAD, width), BF16),
        compiler_params=VMEM,
    )(received, query_map, key_map)
    blocks = pl.pallas_call(
        functools.partial(blocks_kernel, key_scale),
        in_specs=[whole] * 3,
        out_shape=jax.ShapeDtypeStruct((near, share, 2 * width, width), BF16),
        cost_estimate=pl.CostEstimate(flops=2 * flops, bytes_accessed=2 << 20, transcendentals=0),
        compiler_params=VMEM,
    )(received, query_map, key_map)
    got = lax.ppermute(send, "core", swap)
    keep, send = pl.pallas_call(
        halve_kernel, in_specs=[whole] * 2, out_shape=[part] * 2, compiler_params=VMEM
    )(keep, got)
    totals = exchange(totals, "outer")
    totals, send = lax.optimization_barrier((totals, send))
    inside_got = lax.ppermute(send, "y_lo", swap)
    states, owned = pl.pallas_call(
        functools.partial(spread_kernel, key_scale, map_scale),
        in_specs=[whole] * 3,
        out_shape=[
            jax.ShapeDtypeStruct((near, rows, width), BF16),
            jax.ShapeDtypeStruct((2, near, 32, width), BF16),
        ],
        compiler_params=VMEM,
    )(received, blocks, totals)
    carried = exchange(states, NEAR)
    maps = pl.pallas_call(
        pair_kernel,
        in_specs=[whole] * 4,
        out_shape=jax.ShapeDtypeStruct((near, quarter + 32, width), BF16),
        compiler_params=VMEM,
    )(keep, inside_got, owned, lax.ppermute(owned[1], "core", swap))
    carried, maps = lax.optimization_barrier((carried, maps))
    query_grad, key_grad, value_grad = pl.pallas_call(
        functools.partial(grads_kernel, key_scale),
        grid=(steps,),
        in_specs=[wide] * 4 + [gate_spec, map_spec, map_spec] + [wide] * 2
        + [pl.BlockSpec((near // steps, rows, width), lambda i: (i, 0, 0))],
        out_specs=[wide] * 3,
        out_shape=[wide_shape] * 3,
        cost_estimate=pl.CostEstimate(flops=7 * flops, bytes_accessed=8 << 20, transcendentals=0),
    )(v, g, fq, fk, gates, query_map, key_map, query_inside, key_inside, carried)
    maps, query_grad = lax.optimization_barrier((exchange(maps, NEAR), query_grad))
    maps = pl.pallas_call(
        gather_kernel,
        in_specs=[whole],
        out_shape=jax.ShapeDtypeStruct((2, 2, 2, 32, width), BF16),
        compiler_params=VMEM,
    )(maps)
    maps = exchange(maps.reshape(32, 8, width), ("y_hi", "y_lo", "outer"))
    map_grads = add_up(maps, F32)
    shape = queries.shape
    return query_grad.reshape(shape), key_grad.reshape(shape), value_grad.reshape(shape), map_grads


def solution(mesh):
    fine = Mesh(np.asarray(mesh.devices).reshape(4, 2, 2, 4, 2, 4), DP + CONTEXT)
    split = P(DP, CONTEXT, None)

    return jax.shard_map(
        per_device,
        mesh=fine,
        in_specs=(split, split, split, split, P(DP, None, CONTEXT), P(), P()),
        out_specs=(split, split, split, P(DP + CONTEXT, None)),
        check_vma=False,
    )
```

```python
import functools

import jax
import jax.numpy as jnp
import numpy as np
from jax import lax
from jax.experimental import pallas as pl
from jax.experimental.pallas import tpu as pltpu
from jax.sharding import Mesh, PartitionSpec as P

F32 = jnp.float32
BF16 = jnp.bfloat16
GROUP = 8
PAD = 8
DP = ("y_hi", "y_lo", "core")
CONTEXT = ("outer", "inner", "x")
NEAR = ("inner", "x")
VMEM = pltpu.CompilerParams(vmem_limit_bytes=20 << 20)


def dot(a, b, contract, precision=None):
    return lax.dot_general(
        a, b, ((contract[:1], contract[1:]), ((), ())), precision=precision, preferred_element_type=F32
    )


def place(head):
    return 2 * (head // 4) + head % 2, (head // 2) % 2


def causal_mask(length):
    t = lax.broadcasted_iota(jnp.int32, (length, length), 0)
    s = lax.broadcasted_iota(jnp.int32, (length, length), 1)
    return t >= s


def running_columns(gates):
    lower = jnp.where(causal_mask(gates.shape[1]), 1.0, 0.0).astype(F32)
    return dot(lower, gates, (1, 1), lax.Precision.HIGHEST)


def running_rows(gates):
    lower = jnp.where(causal_mask(gates.shape[1]), 1.0, 0.0).astype(F32)
    return dot(gates, lower, (1, 1), lax.Precision.HIGHEST)


def products_kernel(q_ref, k_ref, v_ref, g_ref, gates_ref, out_ref):
    length = q_ref.shape[0]
    width = q_ref.shape[1] // GROUP
    columns = running_columns(gates_ref[...])
    for j in range(GROUP):
        lanes = slice(j * width, (j + 1) * width)
        owner, bit = place(j)
        run = columns[:, j : j + 1]
        closing = run[length - 1 : length]
        g_start = (g_ref[:, lanes].astype(F32) * jnp.exp(run)).astype(BF16)
        v_end = (v_ref[:, lanes].astype(F32) * jnp.exp(closing - run)).astype(BF16)
        to = 2 * owner + bit
        out_ref[to, 0:width] = dot(q_ref[:, lanes], g_start, (0, 0)).astype(BF16)
        out_ref[to, width : 2 * width] = dot(k_ref[:, lanes], v_end, (0, 0)).astype(BF16)
        out_ref[to, 2 * width :] = jnp.broadcast_to(closing, (PAD, width)).astype(BF16)


def owned_heads():
    x = lax.axis_index("x")
    return (lax.axis_index("inner") * 2 + x // 2) * 4 + x % 2


def inside_kernel(
    key_scale, map_scale, q_ref, k_ref, v_ref, g_ref, gates_ref, mq_ref, mk_ref,
    fq_ref, fk_ref, qb_ref, kb_ref, keep_ref, send_ref, maps_ref, sems,
):
    heads, width = mq_ref.shape[0], mq_ref.shape[1]
    step = pl.program_id(0)
    causal = causal_mask(q_ref.shape[0])
    columns = running_columns(gates_ref[...])
    rows = running_rows(gates_ref[...])
    for j in range(heads):
        lanes = slice(j * width, (j + 1) * width)
        owner, bit = place(j)
        within = jnp.exp(jnp.where(causal, columns[:, j : j + 1] - rows[j : j + 1], -1e30))
        q, k, v, g = q_ref[:, lanes], k_ref[:, lanes], v_ref[:, lanes], g_ref[:, lanes]
        fq = dot(q, mq_ref[j], (1, 0)).astype(BF16)
        fk = (dot(k, mk_ref[j], (1, 0)) * key_scale).astype(BF16)
        grad_scores = (dot(g, v, (1, 1)) * within).astype(BF16)
        query_back = dot(grad_scores, fk, (1, 0))
        key_back = dot(grad_scores, fq, (0, 0)) * key_scale
        fq_ref[:, lanes] = fq
        fk_ref[:, lanes] = fk
        qb_ref[:, lanes] = query_back
        kb_ref[:, lanes] = key_back
        for m, (x, back) in enumerate(((q, query_back), (k, key_back))):
            part = dot(x, back.astype(BF16), (0, 0)) * map_scale
            for b in range(width // 8):
                to = (owner % 2) * 16 + (b // 8) * 8
                maps_ref[bit, (owner // 2) % 2, b % 8, m, step, to : to + 8] = part[8 * b : 8 * b + 8].astype(BF16)

    @pl.when(step == pl.num_programs(0) - 1)
    def _():
        core, y_lo = lax.axis_index("core"), lax.axis_index("y_lo")
        copies = []
        for side in range(2):
            along = lax.bitwise_xor(y_lo, side)
            for to, (ref, of) in enumerate(((keep_ref, core), (send_ref, 1 - core))):
                copies.append(pltpu.make_async_copy(maps_ref.at[of, along], ref.at[side], sems.at[2 * side + to]))
        for copy in copies:
            copy.start()
        for copy in copies:
            copy.wait()


def over(decay, value):
    rows, width = value.shape
    return (decay[None] * value.reshape(rows // PAD, PAD, width)).reshape(rows, width)


def decay_of(ref, r, h, width):
    return jnp.exp(ref[r, h, 2 * width :].astype(F32))


def block_state(key_scale, in_ref, map_ref, head, r, h, width):
    return dot(map_ref[head], in_ref[r, h, width : 2 * width], (0, 0)) * key_scale


def block_grad(in_ref, map_ref, head, r, h, width):
    return dot(map_ref[head], in_ref[r, h, 0:width], (0, 0))


def totals_kernel(key_scale, in_ref, mq_ref, mk_ref, out_ref):
    near, heads, width = in_ref.shape[0], in_ref.shape[1], in_ref.shape[3]
    mine = lax.axis_index("outer")
    for h in range(heads):
        head = owned_heads() + 2 * h
        ahead = jnp.zeros((width, width), F32)
        back = jnp.zeros((width, width), F32)
        log = jnp.zeros((PAD, width), F32)
        for r in range(near):
            b = near - 1 - r
            state = block_state(key_scale, in_ref, mk_ref, head, r, h, width)
            ahead = over(decay_of(in_ref, r, h, width), ahead) + state
            back = over(decay_of(in_ref, b, h, width), back) + block_grad(in_ref, mq_ref, head, b, h, width)
            log = log + in_ref[r, h, 2 * width :].astype(F32)
        coarse = log.astype(BF16)
        fine = (log - coarse.astype(F32)).astype(BF16)
        for o in range(out_ref.shape[0]):
            out_ref[o, h, 0:width] = jnp.where(o > mine, ahead, back).astype(BF16)
            out_ref[o, h, width : width + PAD] = coarse
            out_ref[o, h, width + PAD :] = fine


def blocks_kernel(key_scale, in_ref, mq_ref, mk_ref, out_ref):
    near, heads, width = in_ref.shape[0], in_ref.shape[1], in_ref.shape[3]
    for h in range(heads):
        head = owned_heads() + 2 * h
        for r in range(near):
            out_ref[r, h, 0:width] = block_state(key_scale, in_ref, mk_ref, head, r, h, width).astype(BF16)
            out_ref[r, h, width:] = block_grad(in_ref, mq_ref, head, r, h, width).astype(BF16)


def spread_kernel(key_scale, map_scale, in_ref, blocks_ref, totals_ref, states_ref, maps_ref):
    near, heads, width = in_ref.shape[0], in_ref.shape[1], in_ref.shape[3]
    groups = totals_ref.shape[0]
    mine, core = lax.axis_index("outer"), lax.axis_index("core")

    def total(o, h):
        log = totals_ref[o, h, width : width + PAD].astype(F32) + totals_ref[o, h, width + PAD :].astype(F32)
        return jnp.exp(log), totals_ref[o, h, 0:width].astype(F32)

    for h in range(heads):
        ahead = jnp.zeros((width, width), F32)
        back = jnp.zeros((width, width), F32)
        for o in range(groups):
            decay, value = total(o, h)
            ahead = jnp.where(o < mine, over(decay, ahead) + value, ahead)
            b = groups - 1 - o
            decay, value = total(b, h)
            back = jnp.where(b > mine, over(decay, back) + value, back)
        sums = [jnp.zeros((width, width), F32), jnp.zeros((width, width), F32)]
        for r in range(near):
            b = near - 1 - r
            state_in, grad_in = ahead.astype(BF16), back.astype(BF16)
            states_ref[r, 2 * h * width : (2 * h + 1) * width] = state_in
            states_ref[b, (2 * h + 1) * width : (2 * h + 2) * width] = grad_in
            sums[0] = sums[0] + dot(in_ref[r, h, 0:width], state_in, (1, 1))
            sums[1] = sums[1] + dot(in_ref[b, h, width : 2 * width], grad_in, (1, 1))
            if r < near - 1:
                ahead = over(decay_of(in_ref, r, h, width), ahead) + blocks_ref[r, h, 0:width].astype(F32)
                back = over(decay_of(in_ref, b, h, width), back) + blocks_ref[b, h, width:].astype(F32)
        side = lax.bitwise_xor(core, h)
        for m, scale in enumerate((map_scale, map_scale * key_scale)):
            part = sums[m] * scale
            for b in range(width // 8):
                to = (m * 2 + b // 8) * 8
                maps_ref[side, b % 8, to : to + 8] = part[8 * b : 8 * b + 8].astype(BF16)


def halve_kernel(kept_ref, got_ref, keep_ref, send_ref):
    keep_ref[...] = (kept_ref[0].astype(F32) + got_ref[0].astype(F32)).astype(BF16)
    send_ref[...] = (kept_ref[1].astype(F32) + got_ref[1].astype(F32)).astype(BF16)


def pair_kernel(inside_ref, inside_got_ref, carried_ref, carried_got_ref, out_ref):
    rows = inside_ref.shape[1]
    out_ref[:, 0:rows] = (inside_ref[...].astype(F32) + inside_got_ref[...].astype(F32)).astype(BF16)
    out_ref[:, rows:] = (carried_ref[0].astype(F32) + carried_got_ref[...].astype(F32)).astype(BF16)


def gather_kernel(in_ref, out_ref):
    y_lo = lax.axis_index("y_lo")
    rows = in_ref.shape[1] - 32
    for r in range(in_ref.shape[0]):
        for m in range(2):
            of, to = rows + m * 16, (r % 2) * 16
            out_ref[m, r // 4, (r // 2) % 2, to : to + 16] = in_ref[r, of : of + 16]
    total = jnp.sum(in_ref[:, 0:rows].astype(F32), axis=0)
    for m in range(2):
        for high in range(2):
            at = (m * 2 + high) * 32
            here = out_ref[m, high, y_lo].astype(F32)
            out_ref[m, high, y_lo] = (here + total[at : at + 32]).astype(BF16)


def grads_kernel(
    key_scale, v_ref, g_ref, fq_ref, fk_ref, gates_ref, mq_ref, mk_ref, qb_ref, kb_ref, in_ref, qg_ref, kg_ref, vg_ref
):
    width = mq_ref.shape[1]
    length = fk_ref.shape[0]
    causal = causal_mask(length)
    columns = running_columns(gates_ref[...])
    rows = running_rows(gates_ref[...])
    for j in range(GROUP):
        lanes = slice(j * width, (j + 1) * width)
        owner, bit = place(j)
        run = columns[:, j : j + 1]
        within = jnp.exp(jnp.where(causal, run - rows[j : j + 1], -1e30))
        start = jnp.exp(run)
        end = jnp.exp(run[length - 1 : length] - run)
        state_in = in_ref[owner, 2 * bit * width : (2 * bit + 1) * width]
        grad_in = in_ref[owner, (2 * bit + 1) * width : (2 * bit + 2) * width]
        g, fk = g_ref[:, lanes], fk_ref[:, lanes]
        scores = (dot(fq_ref[:, lanes], fk, (1, 1)) * within).astype(BF16)
        query_back = (qb_ref[:, lanes] + dot(g, state_in, (1, 1)) * start).astype(BF16)
        key_back = (kb_ref[:, lanes] + dot(v_ref[:, lanes], grad_in, (1, 1)) * (end * key_scale)).astype(BF16)
        vg_ref[:, lanes] = (dot(scores, g, (0, 0)) + dot(fk, grad_in, (1, 0)) * end).astype(BF16)
        qg_ref[:, lanes] = dot(query_back, mq_ref[j], (1, 1)).astype(BF16)
        kg_ref[:, lanes] = dot(key_back, mk_ref[j], (1, 1)).astype(BF16)


def sum_kernel(in_ref, out_ref):
    out_ref[...] = jnp.sum(in_ref[...].astype(F32), axis=0).astype(out_ref.dtype)


def add_up(value, dtype):
    out_shape = jax.ShapeDtypeStruct(value.shape[1:], dtype)
    return pl.pallas_call(sum_kernel, out_shape=out_shape, compiler_params=VMEM)(value)


def exchange(value, axes):
    return lax.all_to_all(value, axes, 0, 0, tiled=True)


def per_device(queries, keys, values, out_grad, log_gates, query_map, key_map):
    heads, width = query_map.shape[0], query_map.shape[1]
    length = queries.shape[1]
    near, outer = lax.axis_size(NEAR), lax.axis_size("outer")
    key_scale = width ** (-0.5) / 16.0
    map_scale = (lax.axis_size(DP) * lax.axis_size(CONTEXT) * length) ** (-0.5)
    steps = heads // GROUP
    share = heads // near
    q, k, v, g = (x.reshape(length, heads * width) for x in (queries, keys, values, out_grad))
    gates = log_gates.reshape(heads, length)
    wide = pl.BlockSpec((length, GROUP * width), lambda i: (0, i))
    gate_spec = pl.BlockSpec((GROUP, length), lambda i: (i, 0))
    map_spec = pl.BlockSpec((GROUP, width, width), lambda i: (i, 0, 0))
    wide_shape = jax.ShapeDtypeStruct((length, heads * width), BF16)
    sum_shape = jax.ShapeDtypeStruct((length, heads * width), F32)
    flops = 2 * length * width * width * heads
    sent = pl.pallas_call(
        products_kernel,
        grid=(steps,),
        in_specs=[wide, wide, wide, wide, gate_spec],
        out_specs=pl.BlockSpec((GROUP, 2 * width + PAD, width), lambda i: (i, 0, 0)),
        out_shape=jax.ShapeDtypeStruct((heads, 2 * width + PAD, width), BF16),
        cost_estimate=pl.CostEstimate(flops=2 * flops, bytes_accessed=3 << 20, transcendentals=0),
    )(q, k, v, g, gates)
    received = exchange(sent.reshape(near, share, 2 * width + PAD, width), NEAR)
    rows, quarter = 2 * share * width, heads * 8
    half_shape = jax.ShapeDtypeStruct((2, near, 2, steps, 32, width), BF16)
    anywhere = pl.BlockSpec(memory_space=pl.ANY)
    fq, fk, query_inside, key_inside, keep, send = pl.pallas_call(
        functools.partial(inside_kernel, key_scale, map_scale),
        grid=(steps,),
        in_specs=[wide] * 4 + [gate_spec, map_spec, map_spec],
        out_specs=[wide] * 4 + [anywhere] * 2,
        out_shape=[wide_shape] * 2 + [sum_shape] * 2 + [half_shape] * 2,
        scratch_shapes=[pltpu.VMEM((2, 2, near, 2, steps, 32, width), BF16), pltpu.SemaphoreType.DMA((4,))],
        cost_estimate=pl.CostEstimate(flops=7 * flops, bytes_accessed=8 << 20, transcendentals=1 << 18),
    )(q, k, v, g, gates, query_map, key_map)
    keep, send = (x.reshape(2, near, quarter, width) for x in (keep, send))
    received, keep = lax.optimization_barrier((received, keep))
    swap = [(0, 1), (1, 0)]
    whole = pl.BlockSpec(memory_space=pltpu.VMEM)
    part = jax.ShapeDtypeStruct((near, quarter, width), BF16)
    totals = pl.pallas_call(
        functools.partial(totals_kernel, key_scale),
        in_specs=[whole] * 3,
        out_shape=jax.ShapeDtypeStruct((outer, share, width + 2 * PAD, width), BF16),
        compiler_params=VMEM,
    )(received, query_map, key_map)
    blocks = pl.pallas_call(
        functools.partial(blocks_kernel, key_scale),
        in_specs=[whole] * 3,
        out_shape=jax.ShapeDtypeStruct((near, share, 2 * width, width), BF16),
        cost_estimate=pl.CostEstimate(flops=2 * flops, bytes_accessed=2 << 20, transcendentals=0),
        compiler_params=VMEM,
    )(received, query_map, key_map)
    got = lax.ppermute(send, "core", swap)
    keep, send = pl.pallas_call(
        halve_kernel, in_specs=[whole] * 2, out_shape=[part] * 2, compiler_params=VMEM
    )(keep, got)
    totals = exchange(totals, "outer")
    totals, send = lax.optimization_barrier((totals, send))
    inside_got = lax.ppermute(send, "y_lo", swap)
    states, owned = pl.pallas_call(
        functools.partial(spread_kernel, key_scale, map_scale),
        in_specs=[whole] * 3,
        out_shape=[
            jax.ShapeDtypeStruct((near, rows, width), BF16),
            jax.ShapeDtypeStruct((2, near, 32, width), BF16),
        ],
        compiler_params=VMEM,
    )(received, blocks, totals)
    carried = exchange(states, NEAR)
    maps = pl.pallas_call(
        pair_kernel,
        in_specs=[whole] * 4,
        out_shape=jax.ShapeDtypeStruct((near, quarter + 32, width), BF16),
        compiler_params=VMEM,
    )(keep, inside_got, owned, lax.ppermute(owned[1], "core", swap))
    carried, maps = lax.optimization_barrier((carried, maps))

    def grads(part, carried, *written):
        mine = pl.BlockSpec((length, GROUP * width), lambda i: (0, part))
        maps_of = pl.BlockSpec((GROUP, width, width), lambda i: (part, 0, 0))

        def kernel(*refs):
            grads_kernel(key_scale, *refs[:10], *refs[10 + len(written) :])

        return pl.pallas_call(
            kernel,
            grid=(1,),
            in_specs=[mine] * 4 + [pl.BlockSpec((GROUP, length), lambda i: (part, 0)), maps_of, maps_of] + [mine] * 2
            + [pl.BlockSpec((near // steps, rows, width), lambda i: (part, 0, 0))] + [anywhere] * len(written),
            out_specs=[mine] * 3,
            out_shape=[wide_shape] * 3,
            input_output_aliases={10 + i: i for i in range(len(written))},
            cost_estimate=pl.CostEstimate(flops=7 * flops // 2, bytes_accessed=4 << 20, transcendentals=0),
        )(v, g, fq, fk, gates, query_map, key_map, query_inside, key_inside, carried, *written)

    written = grads(0, carried)
    maps, carried, *written = lax.optimization_barrier((exchange(maps, NEAR), carried, *written))
    query_grad, key_grad, value_grad = grads(1, carried, *written)
    maps = pl.pallas_call(
        gather_kernel,
        in_specs=[whole],
        out_shape=jax.ShapeDtypeStruct((2, 2, 2, 32, width), BF16),
        compiler_params=VMEM,
    )(maps)
    maps = exchange(maps.reshape(32, 8, width), ("y_hi", "y_lo", "outer"))
    map_grads = add_up(maps, F32)
    shape = queries.shape
    return query_grad.reshape(shape), key_grad.reshape(shape), value_grad.reshape(shape), map_grads


def solution(mesh):
    fine = Mesh(np.asarray(mesh.devices).reshape(4, 2, 2, 4, 2, 4), DP + CONTEXT)
    split = P(DP, CONTEXT, None)

    return jax.shard_map(
        per_device,
        mesh=fine,
        in_specs=(split, split, split, split, P(DP, None, CONTEXT), P(), P()),
        out_specs=(split, split, split, P(DP + CONTEXT, None)),
        check_vma=False,
    )
```

```python
import functools

import jax
import jax.numpy as jnp
import numpy as np
from jax import lax
from jax.experimental import pallas as pl
from jax.experimental.pallas import tpu as pltpu
from jax.sharding import Mesh, PartitionSpec as P

F32 = jnp.float32
BF16 = jnp.bfloat16
GROUP = 8
PAD = 8
DP = ("y_hi", "y_lo", "core")
CONTEXT = ("outer", "inner", "x")
NEAR = ("inner", "x")
VMEM = pltpu.CompilerParams(vmem_limit_bytes=20 << 20)


def dot(a, b, contract, precision=None):
    return lax.dot_general(
        a, b, ((contract[:1], contract[1:]), ((), ())), precision=precision, preferred_element_type=F32
    )


def place(head):
    return 2 * (head // 4) + head % 2, (head // 2) % 2


def causal_mask(length):
    t = lax.broadcasted_iota(jnp.int32, (length, length), 0)
    s = lax.broadcasted_iota(jnp.int32, (length, length), 1)
    return t >= s


def running_columns(gates):
    lower = jnp.where(causal_mask(gates.shape[1]), 1.0, 0.0).astype(F32)
    return dot(lower, gates, (1, 1), lax.Precision.HIGHEST)


def running_rows(gates):
    lower = jnp.where(causal_mask(gates.shape[1]), 1.0, 0.0).astype(F32)
    return dot(gates, lower, (1, 1), lax.Precision.HIGHEST)


def products_kernel(q_ref, k_ref, v_ref, g_ref, gates_ref, out_ref):
    length = q_ref.shape[0]
    width = q_ref.shape[1] // GROUP
    columns = running_columns(gates_ref[...])
    for j in range(GROUP):
        lanes = slice(j * width, (j + 1) * width)
        owner, bit = place(j)
        run = columns[:, j : j + 1]
        closing = run[length - 1 : length]
        g_start = (g_ref[:, lanes].astype(F32) * jnp.exp(run)).astype(BF16)
        v_end = (v_ref[:, lanes].astype(F32) * jnp.exp(closing - run)).astype(BF16)
        to = 2 * owner + bit
        out_ref[to, 0:width] = dot(q_ref[:, lanes], g_start, (0, 0)).astype(BF16)
        out_ref[to, width : 2 * width] = dot(k_ref[:, lanes], v_end, (0, 0)).astype(BF16)
        out_ref[to, 2 * width :] = jnp.broadcast_to(closing, (PAD, width)).astype(BF16)


def owned_heads():
    x = lax.axis_index("x")
    return (lax.axis_index("inner") * 2 + x // 2) * 4 + x % 2


def inside_kernel(
    key_scale, map_scale, q_ref, k_ref, v_ref, g_ref, gates_ref, mq_ref, mk_ref,
    fq_ref, fk_ref, qb_ref, kb_ref, keep_ref, send_ref, maps_ref, sems,
):
    heads, width = mq_ref.shape[0], mq_ref.shape[1]
    step = pl.program_id(0)
    causal = causal_mask(q_ref.shape[0])
    columns = running_columns(gates_ref[...])
    rows = running_rows(gates_ref[...])
    for j in range(heads):
        lanes = slice(j * width, (j + 1) * width)
        owner, bit = place(j)
        within = jnp.exp(jnp.where(causal, columns[:, j : j + 1] - rows[j : j + 1], -1e30))
        q, k, v, g = q_ref[:, lanes], k_ref[:, lanes], v_ref[:, lanes], g_ref[:, lanes]
        fq = dot(q, mq_ref[j], (1, 0)).astype(BF16)
        fk = (dot(k, mk_ref[j], (1, 0)) * key_scale).astype(BF16)
        grad_scores = (dot(g, v, (1, 1)) * within).astype(BF16)
        query_back = dot(grad_scores, fk, (1, 0))
        key_back = dot(grad_scores, fq, (0, 0)) * key_scale
        fq_ref[:, lanes] = fq
        fk_ref[:, lanes] = fk
        qb_ref[:, lanes] = query_back
        kb_ref[:, lanes] = key_back
        for m, (x, back) in enumerate(((q, query_back), (k, key_back))):
            part = dot(x, back.astype(BF16), (0, 0)) * map_scale
            for b in range(width // 8):
                to = (owner % 2) * 16 + (b // 8) * 8
                maps_ref[bit, (owner // 2) % 2, b % 8, m, step, to : to + 8] = part[8 * b : 8 * b + 8].astype(BF16)

    @pl.when(step == pl.num_programs(0) - 1)
    def _():
        core, y_lo = lax.axis_index("core"), lax.axis_index("y_lo")
        copies = []
        for side in range(2):
            along = lax.bitwise_xor(y_lo, side)
            for to, (ref, of) in enumerate(((keep_ref, core), (send_ref, 1 - core))):
                copies.append(pltpu.make_async_copy(maps_ref.at[of, along], ref.at[side], sems.at[2 * side + to]))
        for copy in copies:
            copy.start()
        for copy in copies:
            copy.wait()


def over(decay, value):
    rows, width = value.shape
    return (decay[None] * value.reshape(rows // PAD, PAD, width)).reshape(rows, width)


def decay_of(ref, r, h, width):
    return jnp.exp(ref[r, h, 2 * width :].astype(F32))


def block_state(key_scale, in_ref, map_ref, head, r, h, width):
    return dot(map_ref[head], in_ref[r, h, width : 2 * width], (0, 0)) * key_scale


def block_grad(in_ref, map_ref, head, r, h, width):
    return dot(map_ref[head], in_ref[r, h, 0:width], (0, 0))


def totals_kernel(key_scale, in_ref, mq_ref, mk_ref, out_ref):
    near, heads, width = in_ref.shape[0], in_ref.shape[1], in_ref.shape[3]
    mine = lax.axis_index("outer")
    for h in range(heads):
        head = owned_heads() + 2 * h
        ahead = jnp.zeros((width, width), F32)
        back = jnp.zeros((width, width), F32)
        log = jnp.zeros((PAD, width), F32)
        for r in range(near):
            b = near - 1 - r
            state = block_state(key_scale, in_ref, mk_ref, head, r, h, width)
            ahead = over(decay_of(in_ref, r, h, width), ahead) + state
            back = over(decay_of(in_ref, b, h, width), back) + block_grad(in_ref, mq_ref, head, b, h, width)
            log = log + in_ref[r, h, 2 * width :].astype(F32)
        coarse = log.astype(BF16)
        fine = (log - coarse.astype(F32)).astype(BF16)
        for o in range(out_ref.shape[0]):
            out_ref[o, h, 0:width] = jnp.where(o > mine, ahead, back).astype(BF16)
            out_ref[o, h, width : width + PAD] = coarse
            out_ref[o, h, width + PAD :] = fine


def blocks_kernel(key_scale, in_ref, mq_ref, mk_ref, out_ref):
    near, heads, width = in_ref.shape[0], in_ref.shape[1], in_ref.shape[3]
    for h in range(heads):
        head = owned_heads() + 2 * h
        for r in range(near):
            out_ref[r, h, 0:width] = block_state(key_scale, in_ref, mk_ref, head, r, h, width).astype(BF16)
            out_ref[r, h, width:] = block_grad(in_ref, mq_ref, head, r, h, width).astype(BF16)


def spread_kernel(key_scale, map_scale, in_ref, blocks_ref, totals_ref, states_ref, maps_ref):
    near, heads, width = in_ref.shape[0], in_ref.shape[1], in_ref.shape[3]
    groups = totals_ref.shape[0]
    mine, core = lax.axis_index("outer"), lax.axis_index("core")

    def total(o, h):
        log = totals_ref[o, h, width : width + PAD].astype(F32) + totals_ref[o, h, width + PAD :].astype(F32)
        return jnp.exp(log), totals_ref[o, h, 0:width].astype(F32)

    for h in range(heads):
        ahead = jnp.zeros((width, width), F32)
        back = jnp.zeros((width, width), F32)
        for o in range(groups):
            decay, value = total(o, h)
            ahead = jnp.where(o < mine, over(decay, ahead) + value, ahead)
            b = groups - 1 - o
            decay, value = total(b, h)
            back = jnp.where(b > mine, over(decay, back) + value, back)
        sums = [jnp.zeros((width, width), F32), jnp.zeros((width, width), F32)]
        for r in range(near):
            b = near - 1 - r
            state_in, grad_in = ahead.astype(BF16), back.astype(BF16)
            states_ref[r, 2 * h * width : (2 * h + 1) * width] = state_in
            states_ref[b, (2 * h + 1) * width : (2 * h + 2) * width] = grad_in
            sums[0] = sums[0] + dot(in_ref[r, h, 0:width], state_in, (1, 1))
            sums[1] = sums[1] + dot(in_ref[b, h, width : 2 * width], grad_in, (1, 1))
            if r < near - 1:
                ahead = over(decay_of(in_ref, r, h, width), ahead) + blocks_ref[r, h, 0:width].astype(F32)
                back = over(decay_of(in_ref, b, h, width), back) + blocks_ref[b, h, width:].astype(F32)
        side = lax.bitwise_xor(core, h)
        for m, scale in enumerate((map_scale, map_scale * key_scale)):
            part = sums[m] * scale
            for b in range(width // 8):
                to = (m * 2 + b // 8) * 8
                maps_ref[side, b % 8, to : to + 8] = part[8 * b : 8 * b + 8].astype(BF16)


def halve_kernel(kept_ref, got_ref, keep_ref, send_ref):
    keep_ref[...] = (kept_ref[0].astype(F32) + got_ref[0].astype(F32)).astype(BF16)
    send_ref[...] = (kept_ref[1].astype(F32) + got_ref[1].astype(F32)).astype(BF16)


def pair_kernel(inside_ref, inside_got_ref, carried_ref, carried_got_ref, out_ref):
    rows = inside_ref.shape[1]
    out_ref[:, 0:rows] = (inside_ref[...].astype(F32) + inside_got_ref[...].astype(F32)).astype(BF16)
    out_ref[:, rows:] = (carried_ref[0].astype(F32) + carried_got_ref[...].astype(F32)).astype(BF16)


def gather_kernel(in_ref, out_ref):
    y_lo = lax.axis_index("y_lo")
    rows = in_ref.shape[1] - 32
    for r in range(in_ref.shape[0]):
        for m in range(2):
            of, to = rows + m * 16, (r % 2) * 16
            out_ref[m, r // 4, (r // 2) % 2, to : to + 16] = in_ref[r, of : of + 16]
    total = jnp.sum(in_ref[:, 0:rows].astype(F32), axis=0)
    for m in range(2):
        for high in range(2):
            at = (m * 2 + high) * 32
            here = out_ref[m, high, y_lo].astype(F32)
            out_ref[m, high, y_lo] = (here + total[at : at + 32]).astype(BF16)


def values_kernel(g_ref, fq_ref, fk_ref, gates_ref, out_ref):
    width = g_ref.shape[1] // GROUP
    causal = causal_mask(g_ref.shape[0])
    columns = running_columns(gates_ref[...])
    rows = running_rows(gates_ref[...])
    for j in range(GROUP):
        lanes = slice(j * width, (j + 1) * width)
        within = jnp.exp(jnp.where(causal, columns[:, j : j + 1] - rows[j : j + 1], -1e30))
        scores = (dot(fq_ref[:, lanes], fk_ref[:, lanes], (1, 1)) * within).astype(BF16)
        out_ref[:, lanes] = dot(scores, g_ref[:, lanes], (0, 0))


def grads_kernel(
    key_scale, v_ref, g_ref, vgi_ref, fk_ref, gates_ref, mq_ref, mk_ref, qb_ref, kb_ref, in_ref, qg_ref, kg_ref, vg_ref
):
    width = mq_ref.shape[1]
    length = fk_ref.shape[0]
    columns = running_columns(gates_ref[...])
    for j in range(GROUP):
        lanes = slice(j * width, (j + 1) * width)
        owner, bit = place(j)
        run = columns[:, j : j + 1]
        start = jnp.exp(run)
        end = jnp.exp(run[length - 1 : length] - run)
        state_in = in_ref[owner, 2 * bit * width : (2 * bit + 1) * width]
        grad_in = in_ref[owner, (2 * bit + 1) * width : (2 * bit + 2) * width]
        g, fk = g_ref[:, lanes], fk_ref[:, lanes]
        query_back = (qb_ref[:, lanes] + dot(g, state_in, (1, 1)) * start).astype(BF16)
        key_back = (kb_ref[:, lanes] + dot(v_ref[:, lanes], grad_in, (1, 1)) * (end * key_scale)).astype(BF16)
        vg_ref[:, lanes] = (vgi_ref[:, lanes] + dot(fk, grad_in, (1, 0)) * end).astype(BF16)
        qg_ref[:, lanes] = dot(query_back, mq_ref[j], (1, 1)).astype(BF16)
        kg_ref[:, lanes] = dot(key_back, mk_ref[j], (1, 1)).astype(BF16)


def sum_kernel(in_ref, out_ref):
    out_ref[...] = jnp.sum(in_ref[...].astype(F32), axis=0).astype(out_ref.dtype)


def add_up(value, dtype):
    out_shape = jax.ShapeDtypeStruct(value.shape[1:], dtype)
    return pl.pallas_call(sum_kernel, out_shape=out_shape, compiler_params=VMEM)(value)


def exchange(value, axes):
    return lax.all_to_all(value, axes, 0, 0, tiled=True)


def per_device(queries, keys, values, out_grad, log_gates, query_map, key_map):
    heads, width = query_map.shape[0], query_map.shape[1]
    length = queries.shape[1]
    near, outer = lax.axis_size(NEAR), lax.axis_size("outer")
    key_scale = width ** (-0.5) / 16.0
    map_scale = (lax.axis_size(DP) * lax.axis_size(CONTEXT) * length) ** (-0.5)
    steps = heads // GROUP
    share = heads // near
    q, k, v, g = (x.reshape(length, heads * width) for x in (queries, keys, values, out_grad))
    gates = log_gates.reshape(heads, length)
    wide = pl.BlockSpec((length, GROUP * width), lambda i: (0, i))
    gate_spec = pl.BlockSpec((GROUP, length), lambda i: (i, 0))
    map_spec = pl.BlockSpec((GROUP, width, width), lambda i: (i, 0, 0))
    wide_shape = jax.ShapeDtypeStruct((length, heads * width), BF16)
    sum_shape = jax.ShapeDtypeStruct((length, heads * width), F32)
    flops = 2 * length * width * width * heads
    sent = pl.pallas_call(
        products_kernel,
        grid=(steps,),
        in_specs=[wide, wide, wide, wide, gate_spec],
        out_specs=pl.BlockSpec((GROUP, 2 * width + PAD, width), lambda i: (i, 0, 0)),
        out_shape=jax.ShapeDtypeStruct((heads, 2 * width + PAD, width), BF16),
        cost_estimate=pl.CostEstimate(flops=2 * flops, bytes_accessed=3 << 20, transcendentals=0),
    )(q, k, v, g, gates)
    received = exchange(sent.reshape(near, share, 2 * width + PAD, width), NEAR)
    rows, quarter = 2 * share * width, heads * 8
    half_shape = jax.ShapeDtypeStruct((2, near, 2, steps, 32, width), BF16)
    anywhere = pl.BlockSpec(memory_space=pl.ANY)
    fq, fk, query_inside, key_inside, keep, send = pl.pallas_call(
        functools.partial(inside_kernel, key_scale, map_scale),
        grid=(steps,),
        in_specs=[wide] * 4 + [gate_spec, map_spec, map_spec],
        out_specs=[wide] * 4 + [anywhere] * 2,
        out_shape=[wide_shape] * 2 + [sum_shape] * 2 + [half_shape] * 2,
        scratch_shapes=[pltpu.VMEM((2, 2, near, 2, steps, 32, width), BF16), pltpu.SemaphoreType.DMA((4,))],
        cost_estimate=pl.CostEstimate(flops=7 * flops, bytes_accessed=8 << 20, transcendentals=1 << 18),
    )(q, k, v, g, gates, query_map, key_map)
    keep, send = (x.reshape(2, near, quarter, width) for x in (keep, send))
    received, keep = lax.optimization_barrier((received, keep))
    swap = [(0, 1), (1, 0)]
    whole = pl.BlockSpec(memory_space=pltpu.VMEM)
    part = jax.ShapeDtypeStruct((near, quarter, width), BF16)
    totals = pl.pallas_call(
        functools.partial(totals_kernel, key_scale),
        in_specs=[whole] * 3,
        out_shape=jax.ShapeDtypeStruct((outer, share, width + 2 * PAD, width), BF16),
        compiler_params=VMEM,
    )(received, query_map, key_map)
    blocks = pl.pallas_call(
        functools.partial(blocks_kernel, key_scale),
        in_specs=[whole] * 3,
        out_shape=jax.ShapeDtypeStruct((near, share, 2 * width, width), BF16),
        cost_estimate=pl.CostEstimate(flops=2 * flops, bytes_accessed=2 << 20, transcendentals=0),
        compiler_params=VMEM,
    )(received, query_map, key_map)
    got = lax.ppermute(send, "core", swap)
    keep, send = pl.pallas_call(
        halve_kernel, in_specs=[whole] * 2, out_shape=[part] * 2, compiler_params=VMEM
    )(keep, got)
    totals = exchange(totals, "outer")
    totals, send = lax.optimization_barrier((totals, send))
    inside_got = lax.ppermute(send, "y_lo", swap)
    states, owned = pl.pallas_call(
        functools.partial(spread_kernel, key_scale, map_scale),
        in_specs=[whole] * 3,
        out_shape=[
            jax.ShapeDtypeStruct((near, rows, width), BF16),
            jax.ShapeDtypeStruct((2, near, 32, width), BF16),
        ],
        compiler_params=VMEM,
    )(received, blocks, totals)
    value_inside = pl.pallas_call(
        values_kernel,
        grid=(steps,),
        in_specs=[wide] * 3 + [gate_spec],
        out_specs=wide,
        out_shape=sum_shape,
        cost_estimate=pl.CostEstimate(flops=2 * flops, bytes_accessed=3 << 20, transcendentals=1 << 18),
    )(g, fq, fk, gates)
    carried, value_inside = lax.optimization_barrier((exchange(states, NEAR), value_inside))
    maps = pl.pallas_call(
        pair_kernel,
        in_specs=[whole] * 4,
        out_shape=jax.ShapeDtypeStruct((near, quarter + 32, width), BF16),
        compiler_params=VMEM,
    )(keep, inside_got, owned, lax.ppermute(owned[1], "core", swap))
    carried, maps = lax.optimization_barrier((carried, maps))
    query_grad, key_grad, value_grad = pl.pallas_call(
        functools.partial(grads_kernel, key_scale),
        grid=(steps,),
        in_specs=[wide] * 4 + [gate_spec, map_spec, map_spec] + [wide] * 2
        + [pl.BlockSpec((near // steps, rows, width), lambda i: (i, 0, 0))],
        out_specs=[wide] * 3,
        out_shape=[wide_shape] * 3,
        cost_estimate=pl.CostEstimate(flops=5 * flops, bytes_accessed=8 << 20, transcendentals=0),
    )(v, g, value_inside, fk, gates, query_map, key_map, query_inside, key_inside, carried)
    maps, query_grad = lax.optimization_barrier((exchange(maps, NEAR), query_grad))
    maps = pl.pallas_call(
        gather_kernel,
        in_specs=[whole],
        out_shape=jax.ShapeDtypeStruct((2, 2, 2, 32, width), BF16),
        compiler_params=VMEM,
    )(maps)
    maps = exchange(maps.reshape(32, 8, width), ("y_hi", "y_lo", "outer"))
    map_grads = add_up(maps, F32)
    shape = queries.shape
    return query_grad.reshape(shape), key_grad.reshape(shape), value_grad.reshape(shape), map_grads


def solution(mesh):
    fine = Mesh(np.asarray(mesh.devices).reshape(4, 2, 2, 4, 2, 4), DP + CONTEXT)
    split = P(DP, CONTEXT, None)

    return jax.shard_map(
        per_device,
        mesh=fine,
        in_specs=(split, split, split, split, P(DP, None, CONTEXT), P(), P()),
        out_specs=(split, split, split, P(DP + CONTEXT, None)),
        check_vma=False,
    )
```
